32 devices in a mesh: dp: 16 (over z, y, core), seq: 2 (over x).
Axes of the slice: x: 2, y: 2, z: 4, core: 2. Of those that a mesh axis runs over, the one named last changes fastest.
Arguments:
- pre_act: bfloat16 [16, 512, 768], P('dp', 'seq'), may hold values from -6 to 6
- trunk_grad: bfloat16 [16, 256, 768], P('dp', None, 'seq'), may hold values from -6 to 6
- conv_weight: bfloat16 [5, 768, 768], P(None, 'dp'), may hold values from -0.09375 to 0.09375
- pair_weight: bfloat16 [768, 768], replicated, may hold values from -0.21875 to 0.21875
- donor_slots: int32 [16, 2, 2, 128], P('dp', 'seq'), may hold values from 0 to 255
- accept_slots: int32 [16, 2, 2, 128], P('dp', 'seq'), may hold values from 0 to 255
- junction_grad: float32 [16, 2, 2, 128], P('dp', 'seq'), may hold values from -6 to 6
- pair_counts: int32 [16, 2, 2], P('dp'), may hold values from 0 to 128, as said below
Outputs:
- input_grad: bfloat16 [16, 512, 768], P('dp', 'seq')
- pair_grad: float32 [768, 768], replicated
The draws below stay inside these ranges and needn't reach their ends.
Inputs may be any that keep to these rules, and one draw needn't show every extreme that they name: pair_counts is at most 128; in every sample some acceptor slab has 128 live slots from every donor slab.
All inputs are finite; a program needn't handle non-finite values.
Results may differ from the reference program's by a relative error of at most 0.0061.
Values may be sent and summed in bfloat16 or wider, within the bound.
A program may use at most 64 MiB of HBM per device.

```python
import math
import jax
import jax.numpy as jnp
from jax import lax

CHANNELS = 768
KERNEL = 5
SLOTS = 128
SLAB = 256
SAMPLES = 16
SEQ_LEN = 512
TOKENS = 256
JUNCTION_SLOTS = 8192
N_SEQ = 2


def draw_pair_counts(key, part):
    first, second, third = jax.random.split(jax.random.fold_in(key, 11), 3)
    left = jax.random.randint(first, (SAMPLES, N_SEQ, N_SEQ), 0, SLOTS + 1)
    right = jax.random.randint(second, (SAMPLES, N_SEQ, N_SEQ), 0, SLOTS + 1)
    counts = jnp.maximum(left, right)
    full_col = jax.random.randint(third, (SAMPLES,), 0, N_SEQ)
    column = jnp.arange(N_SEQ, dtype=jnp.int32)[None, None, :]
    counts = jnp.where(column == full_col[:, None, None], SLOTS, counts)
    return counts.astype(jnp.int32)


def plant(result, key, low, largest):
    extent = result.shape
    spot = [jax.random.randint(jax.random.fold_in(key, axis), (), 0, extent[axis]) for axis in range(len(extent))]
    result = result.at[tuple(spot)].set(low)
    longest = extent.index(max(extent))
    spot[longest] = (spot[longest] + 1) % extent[longest]
    return result.at[tuple(spot)].set(largest)


def block_scale(key, shape, shards, least, largest):
    loudness = 1.0
    for position, shards_of in shards:
        steps = jax.random.uniform(jax.random.fold_in(jax.random.fold_in(key, 6), position), (shards_of,), jnp.float32, least / len(shards), largest / len(shards))
        loudness = loudness * jnp.repeat(jnp.exp(steps), shape[position] // shards_of).reshape((-1,) + (1,) * (len(shape) - 1 - position))
    return loudness


def scatter_about(key, dims, deviation, reach, cuts=(), kind=jnp.bfloat16):
    drawn = jax.random.normal(key, dims, jnp.float32) * deviation
    if len(cuts) > 0:
        drawn = block_scale(key, dims, cuts, -0.22, 0.18) * drawn
    return jnp.clip(drawn, min=-reach, max=reach).astype(kind)


def setup_inputs(seed: int = 0) -> dict:
    splits = jax.random.split(jax.random.key(seed), 9)
    pre_act = scatter_about(splits[0], (SAMPLES, SEQ_LEN, CHANNELS), 1.0, 6.0, ((0, 16), (1, 2)))
    trunk_grad = scatter_about(splits[1], (SAMPLES, TOKENS, CHANNELS), 1.0, 6.0, ((0, 16), (2, 2)))
    conv_weight = scatter_about(splits[2], (KERNEL, CHANNELS, CHANNELS), (KERNEL * CHANNELS) ** -0.5, 0.09375, ((1, 16),))
    pair_weight = scatter_about(splits[3], (CHANNELS, CHANNELS), CHANNELS ** -0.5, 0.21875)
    donor_slots = plant(jax.random.randint(splits[4], (SAMPLES, N_SEQ, N_SEQ, SLOTS), 0, SLAB), jax.random.fold_in(splits[4], 1), 0, SLAB - 1).astype(jnp.int32)
    accept_slots = plant(jax.random.randint(splits[5], (SAMPLES, N_SEQ, N_SEQ, SLOTS), 0, SLAB), jax.random.fold_in(splits[5], 1), 0, SLAB - 1).astype(jnp.int32)
    junction_grad = scatter_about(splits[6], (SAMPLES, N_SEQ, N_SEQ, SLOTS), 1.0, 6.0, ((0, 16), (1, 2)), jnp.float32)
    pair_counts = draw_pair_counts(jax.random.fold_in(splits[8], 71), 0)
    return dict(pre_act=pre_act, trunk_grad=trunk_grad, conv_weight=conv_weight, pair_weight=pair_weight, donor_slots=donor_slots, accept_slots=accept_slots, junction_grad=junction_grad, pair_counts=pair_counts)


def gelu_parts(values):
    normal_cdf = 0.5 * (1.0 + jax.scipy.special.erf(values / math.sqrt(2.0)))
    density = jnp.exp(-0.5 * values * values) / math.sqrt(2.0 * math.pi)
    return (values * normal_cdf, normal_cdf + values * density)

def per_sample(carry, inputs):
    pre, grad_tok, donors, accepts, weights_in, counts, conv_weight, pair_weight = inputs
    act_f, slope = gelu_parts(pre.astype(jnp.float32))
    act = act_f.astype(jnp.bfloat16)
    pooled = jnp.repeat(grad_tok.astype(jnp.float32) * 0.5, 2, axis=0)
    offsets = jnp.arange(N_SEQ, dtype=jnp.int32) * SLAB
    donor_glob = (jnp.transpose(donors, (1, 0, 2)) + offsets[None, :, None]).reshape(-1).astype(jnp.int32)
    accept_glob = (accepts + offsets[:, None, None]).reshape(-1).astype(jnp.int32)
    live = jnp.arange(SLOTS, dtype=jnp.int32)[None, None, :] < jnp.transpose(counts)[:, :, None]
    slot_w = jnp.where(live, weights_in, 0.0).reshape(-1)
    donor_rows = act[donor_glob]
    accept_rows = act[accept_glob]
    weighted = (slot_w[:, None] * accept_rows.astype(jnp.float32)).astype(jnp.bfloat16)
    accept_term = jnp.dot(donor_rows, pair_weight, preferred_element_type=jnp.float32) * slot_w[:, None]
    donor_term = lax.dot_general(weighted, pair_weight, (((1,), (1,)), ((), ())), preferred_element_type=jnp.float32).astype(jnp.bfloat16)
    pair_part = lax.dot_general(donor_rows, weighted, (((0,), (0,)), ((), ())), preferred_element_type=jnp.float32)
    act_grad = pooled.at[accept_glob].add(accept_term).at[donor_glob].add(donor_term.astype(jnp.float32))
    conv_grad = (act_grad * slope).astype(jnp.bfloat16)
    half = KERNEL // 2
    padded = jnp.pad(conv_grad, ((half, half), (0, 0)))
    total = jnp.zeros((SEQ_LEN, CHANNELS), jnp.float32)
    for tap in range(KERNEL):
        window = padded[2 * half - tap:2 * half - tap + SEQ_LEN]
        total = total + lax.dot_general(window, conv_weight[tap], (((1,), (1,)), ((), ())), preferred_element_type=jnp.float32)
    return (carry + pair_part, total.astype(jnp.bfloat16))

def reference(pre_act, trunk_grad, conv_weight, pair_weight, donor_slots, accept_slots, junction_grad, pair_counts):

    def step(carry, inputs):
        pre, grad_tok, donors, accepts, weights_in, counts = inputs
        return per_sample(carry, (pre, grad_tok, donors, accepts, weights_in, counts, conv_weight, pair_weight))
    start = jnp.zeros((CHANNELS, CHANNELS), jnp.float32)
    pair_sum, input_grad = lax.scan(step, start, (pre_act, trunk_grad, donor_slots, accept_slots, junction_grad, pair_counts))
    pair_grad = pair_sum * (1.0 / math.sqrt(JUNCTION_SLOTS))
    return (input_grad, pair_grad)
```

```python
import math

import jax
import jax.numpy as jnp
from jax import lax
from jax.experimental import pallas as pl
from jax.experimental.pallas import tpu as pltpu
from jax.sharding import PartitionSpec as P


def with_halo(x, sides, width):
    for axis, dim in sides:
        size, length = (lax.axis_size(axis), x.shape[dim])
        up = [(i, (i + 1) % size) for i in range(size - 1)]
        down = [(j, i) for i, j in up]
        last = lax.slice_in_dim(x, length - width, length, axis=dim)
        first = lax.slice_in_dim(x, 0, width, axis=dim)
        before = lax.ppermute(last, axis, up)
        after = lax.ppermute(first, axis, down)
        x = jnp.concatenate([before, x, after], axis=dim)
    return x


def gelu_parts(values):
    normal_cdf = 0.5 * (1.0 + jax.scipy.special.erf(values / math.sqrt(2.0)))
    density = jnp.exp(-0.5 * values * values) / math.sqrt(2.0 * math.pi)
    return (values * normal_cdf, normal_cdf + values * density)


def per_device_general(
    pre_act,
    trunk_grad,
    conv_weight,
    pair_weight,
    donor_slots,
    accept_slots,
    junction_grad,
    pair_counts,
):
    seq_count = lax.axis_size("seq")
    my_slab = lax.axis_index("seq")
    slab_len = pre_act.shape[1]
    channels = pre_act.shape[2]
    slot_count = donor_slots.shape[3]
    kernel = conv_weight.shape[0]
    half = kernel // 2
    act_f, slope = gelu_parts(pre_act[0].astype(jnp.float32))
    act = act_f.astype(jnp.bfloat16)
    arrived = lax.all_to_all(trunk_grad, "seq", split_axis=1, concat_axis=2, tiled=True)
    pooled = jnp.repeat(arrived[0].astype(jnp.float32) * 0.5, 2, axis=0)
    send_index = donor_slots[0, 0].reshape(-1)
    outgoing = act[send_index].reshape(seq_count, slot_count, channels)
    incoming = lax.all_to_all(outgoing, "seq", split_axis=0, concat_axis=0, tiled=True)
    donor_rows = incoming.reshape(-1, channels)
    accept_index = accept_slots[0, 0].reshape(-1)
    counts_in = lax.dynamic_index_in_dim(pair_counts[0], my_slab, axis=1, keepdims=False)
    live = jnp.arange(slot_count, dtype=jnp.int32)[None, :] < counts_in[:, None]
    slot_w = jnp.where(live, junction_grad[0, 0], 0.0).reshape(-1)
    accept_rows = act[accept_index]
    weighted = (slot_w[:, None] * accept_rows.astype(jnp.float32)).astype(jnp.bfloat16)
    accept_term = (
        jnp.dot(donor_rows, pair_weight, preferred_element_type=jnp.float32) * slot_w[:, None]
    )
    donor_term = lax.dot_general(
        weighted, pair_weight, (((1,), (1,)), ((), ())), preferred_element_type=jnp.float32
    ).astype(jnp.bfloat16)
    pair_part = lax.dot_general(
        donor_rows, weighted, (((0,), (0,)), ((), ())), preferred_element_type=jnp.float32
    )
    returned = lax.all_to_all(
        donor_term.reshape(seq_count, slot_count, channels),
        "seq",
        split_axis=0,
        concat_axis=0,
        tiled=True,
    )
    act_grad = (
        pooled.at[accept_index]
        .add(accept_term)
        .at[send_index]
        .add(returned.reshape(-1, channels).astype(jnp.float32))
    )
    conv_grad = (act_grad * slope).astype(jnp.bfloat16)
    padded = with_halo(conv_grad[None], (("seq", 1),), half)[0]
    piece = lax.all_gather(conv_weight, "dp", axis=1, tiled=True)
    total = jnp.zeros((slab_len, piece.shape[1]), jnp.float32)
    for tap in range(kernel):
        window = padded[2 * half - tap : 2 * half - tap + slab_len]
        total = total + lax.dot_general(
            window, piece[tap], (((1,), (1,)), ((), ())), preferred_element_type=jnp.float32
        )
    input_grad = total.astype(jnp.bfloat16)
    pair_sum = lax.psum(pair_part, ("dp", "seq"))
    scale = 1.0 / math.sqrt(lax.axis_size("dp") * seq_count * seq_count * slot_count)
    return (input_grad[None], pair_sum * scale)


MESH = pl.DeviceIdType.MESH
NZ, NY, NC = 4, 2, 2
PEERS = NZ * NY
CHUNKS = 4
ROWS_T = (((0,), (0,)), ((), ()))
COLS_T = (((1,), (1,)), ((), ()))


def dot(a, b):
    return jnp.dot(a, b, preferred_element_type=jnp.float32)


def dot_t(a, b, dims):
    return lax.dot_general(a, b, dims, preferred_element_type=jnp.float32)


def kernel(
    pre_hbm, trunk_hbm, w_ref, p_hbm, ds_hbm, as_hbm, jg_hbm, pc_hbm,
    out_ref, pair_ref,
    pre_s, pcol_s, prow_s, ds_s, as_s, jg_s, pc_s, in_sem,
    act_s, slope_s, idx_send, idx_recv, drows, weighted, zbuf, pad_s, wbuf,
    c_send, c_recv, own_s, r_send, r_recv, r_done, final, o_send, o_recv,
    wz_s, wz_r, wy_s, wy_r, wc_s, wc_r, xs_s, xs_r, cc_s, cc_r,
    rs_s, rs_r, ag_s, ag_r, xf_s, xf_r, ready,
):
    dp = lax.axis_index("dp")
    x = lax.axis_index("seq")
    c = dp % 2
    y = (dp // 2) % 2
    z = dp // 4
    me8 = dp // 2
    ox = 1 - x
    oc = 1 - c
    slab, chan = pre_s.shape[1:]
    slots = ds_s.shape[-1]
    taps, shard = w_ref.shape[:2]
    hc = chan // 2
    tok = slab // 2
    piece = hc // PEERS
    first = x == 0

    def half(index):
        return pl.ds(pl.multiple_of(index * hc, 128), hc)

    mine, theirs = half(x), half(ox)

    def dev(zz, yy, cc):
        return (zz * NY + yy) * NC + cc

    xdev = (dp, ox)
    cdev = (me8 * 2 + oc, x)
    ydev = (dev(z, 1 - y, c), x)

    def zdev(d):
        return (dev(z + 1 if d == 0 else z - 1, y, c), x)

    def has_next(d):
        return z < NZ - 1 if d == 0 else z > 0

    def wpart(index):
        return wbuf.at[:, pl.ds(pl.multiple_of(index * shard, 16), shard), :]

    w_half = w_ref.at[:, :, mine]

    def tokens(s):
        return trunk_hbm.at[0, pl.ds(pl.multiple_of((ox if s else x) * tok, 16), tok), :]

    loads = [
        pltpu.make_async_copy(src, dst, in_sem.at[i])
        for i, (src, dst) in enumerate([
            (ds_hbm, ds_s), (as_hbm, as_s), (jg_hbm, jg_s), (pc_hbm, pc_s),
            (pre_hbm.at[0], pre_s.at[0]),
            (p_hbm.at[:, mine], pcol_s), (p_hbm.at[mine, :], prow_s),
            (tokens(0), zbuf.at[0, 4 * slots :, :]), (tokens(1), zbuf.at[1, 4 * slots :, :]),
            (w_half, wpart(dp))])
    ]
    for cp in loads:
        cp.start()

    barrier = pltpu.get_barrier_semaphore()
    for target in (xdev, cdev, ydev):
        pl.semaphore_signal(barrier, inc=1, device_id=target, device_id_type=MESH)
    for d in range(2):
        @pl.when(has_next(d))
        def _(d=d):
            pl.semaphore_signal(barrier, inc=1, device_id=zdev(d), device_id_type=MESH)

    def remote(src, dst, ss, rs, target):
        return pltpu.make_async_remote_copy(
            src_ref=src, dst_ref=dst, send_sem=ss, recv_sem=rs,
            device_id=target, device_id_type=MESH,
        )

    for cp in loads[:4]:
        cp.wait()

    def ordered(rows):
        a, b = rows[0:1], rows[1:2]
        return [jnp.where(first, a, b), jnp.where(first, b, a)]

    d_own = ordered(ds_s[0, 0].astype(jnp.float32))
    a_own = ordered(as_s[0, 0].astype(jnp.float32))
    counts = pc_s[0]
    cnt = jnp.where(first, counts[:, 0:1], counts[:, 1:2])
    live = lax.broadcasted_iota(jnp.int32, (2, slots), 1) < cnt
    w_own = ordered(jnp.where(live, jg_s[0, 0], 0.0))
    nothing = jnp.zeros((2, slots), jnp.float32)
    idx_send[...] = jnp.concatenate(d_own + a_own + w_own + [nothing], axis=0)

    edge = jnp.where((z == 0) | (z == NZ - 1), 4, 5)
    pl.semaphore_wait(barrier, edge)

    idx_copy = remote(idx_send, idx_recv, xs_s.at[0], xs_r.at[0], xdev)
    idx_copy.start()
    rows_c = slab // CHUNKS
    pre_copies = [
        remote(pre_hbm.at[0, k * rows_c : (k + 1) * rows_c, :],
               pre_s.at[1, k * rows_c : (k + 1) * rows_c, :], xs_s.at[1 + k], xs_r.at[1 + k], xdev)
        for k in range(CHUNKS)]
    for cp in pre_copies:
        cp.start()

    hops = [(d, s) for s in range(NZ - 1) for d in range(2)]

    def entry(hop):
        return 0 if hop is None else 1 + hop[0] * 3 + hop[1]

    def source_z(hop):
        if hop is None:
            return z
        return z - 1 - hop[1] if hop[0] == 0 else z + 1 + hop[1]

    def when(hop, body):
        if hop is None:
            body()
        else:
            pl.when(source_z(hop) >= 0 if hop[0] == 0 else source_z(hop) < NZ)(body)

    def z_copy(d, s):
        block = wpart(dev(z - s if d == 0 else z + s, y, c))
        return remote(w_half if s == 0 else block, block, wz_s.at[d * 3 + s], wz_r.at[d * 3 + s], zdev(d))

    def z_arrival(d, s):
        block = wpart(dev(source_z((d, s)), y, c))
        return remote(block, block, wz_s.at[d * 3 + s], wz_r.at[d * 3 + s], ydev)

    def y_copy(hop, arriving=False):
        block = wpart(dev(source_z(hop), 1 - y if arriving else y, c))
        src = w_half if hop is None and not arriving else block
        return remote(src, block, wy_s.at[entry(hop)], wy_r.at[entry(hop)], ydev)

    def core_copy(kind, hop, arriving=False):
        block = wpart(dev(source_z(hop), 1 - y if kind else y, oc if arriving else c))
        src = w_half if kind == 0 and hop is None and not arriving else block
        sem = kind * 7 + entry(hop)
        return remote(src, block, wc_s.at[sem], wc_r.at[sem], cdev)

    for d in range(2):
        @pl.when(has_next(d))
        def _(d=d):
            z_copy(d, 0).start()
    y_copy(None).start()
    core_copy(0, None).start()

    def say(stage):
        for d in range(2):
            @pl.when(has_next(d))
            def _(d=d):
                pl.semaphore_signal(
                    ready.at[stage * 2 + d], inc=1, device_id=zdev(d), device_id_type=MESH)

    def hear(stage):
        for d in range(2):
            @pl.when(has_next(1 - d))
            def _(d=d):
                pl.semaphore_wait(ready.at[stage * 2 + d], 1)

    say(0)

    def pass_z(s):
        for d in range(2):
            def body(d=d):
                z_arrival(d, s).wait_recv()
                if s < NZ - 2:
                    @pl.when(has_next(d))
                    def _():
                        z_copy(d, s + 1).start()
                y_copy((d, s)).start()
                core_copy(0, (d, s)).start()
            when((d, s), body)

    def pass_y(step):
        for hop in [None] if step == 0 else [(0, step - 1), (1, step - 1)]:
            def body(hop=hop):
                y_copy(hop, True).wait_recv()
                core_copy(1, hop).start()
            when(hop, body)

    def gelu(s, start, count):
        rows = slice(start, start + count)
        for cols in (mine, theirs):
            values = pre_s[s, rows, cols].astype(jnp.float32)
            normal_cdf = 0.5 * (1.0 + lax.erf(values / math.sqrt(2.0)))
            act_s[s, rows, cols] = (values * normal_cdf).astype(jnp.bfloat16)
            if cols is mine:
                slope_s[s, rows, :] = normal_cdf

    def finish_slope(s):
        values = pre_s[s, :, mine].astype(jnp.float32)
        density = jnp.exp(-0.5 * values * values) / math.sqrt(2.0 * math.pi)
        slope_s[s] += values * density

    position = lax.broadcasted_iota(jnp.int32, (slab, 2 * slots), 0).astype(jnp.float32)

    def onehot(pair):
        return jnp.where(position == jnp.concatenate(pair, axis=1), 1.0, 0.0)

    def flip(m):
        return jnp.transpose(m).astype(jnp.bfloat16)

    def column(row):
        return jnp.transpose(jnp.broadcast_to(row, (slots, slots)))[:, 0:1]

    def block(q, r):
        return slice((2 * q + r) * slots, (2 * q + r + 1) * slots)

    def gather_donors(s, hot):
        rows = dot(flip(hot), act_s[s]).astype(jnp.bfloat16)
        for q in range(2):
            drows[block(q, s), :] = rows[q * slots : (q + 1) * slots]

    def gather_acceptors(s, hot, cols):
        rows = dot(flip(hot), act_s[s])
        for r in range(2):
            weighted[block(s, r), :] = (
                cols[r] * rows[r * slots : (r + 1) * slots]).astype(jnp.bfloat16)

    def donor_terms(q):
        term = dot_t(weighted[2 * q * slots : 2 * (q + 1) * slots, :], prow_s[...], COLS_T)
        for r in range(2):
            zbuf[r, (2 + q) * slots : (3 + q) * slots, :] = (
                term[r * slots : (r + 1) * slots].astype(jnp.bfloat16))

    def accept_terms(r, cols):
        for q in range(2):
            term = dot(drows[block(q, r), :], pcol_s[...]) * cols[q][r]
            zbuf[q, r * slots : (r + 1) * slots, :] = term.astype(jnp.bfloat16)

    loads[4].wait()
    gelu(0, 0, slab)
    hot_d = [onehot(d_own)]
    hot_a = [onehot(a_own)]
    w_cols = [[column(w) for w in w_own]]
    gather_donors(0, hot_d[0])
    gather_acceptors(0, hot_a[0], w_cols[0])
    hear(0)
    say(1)
    for cp in loads[5:7]:
        cp.wait()
    donor_terms(0)

    idx_copy.wait_recv()
    got = idx_recv[...]
    hot_d.append(onehot([got[1:2], got[0:1]]))
    hot_a.append(onehot([got[3:4], got[2:3]]))
    w_cols.append([column(got[5:6]), column(got[4:5])])
    accept_terms(0, w_cols)
    finish_slope(0)
    hear(1)
    say(2)
    pass_z(0)
    pass_y(0)
    hear(2)

    for k in range(CHUNKS):
        pre_copies[k].wait_recv()
        gelu(1, k * rows_c, rows_c)
    gather_acceptors(1, hot_a[1], w_cols[1])
    gather_donors(1, hot_d[1])
    c_send[...] = dot_t(drows[:, mine], weighted[:, half(oc)], ROWS_T).astype(jnp.bfloat16)
    c_copy = remote(c_send, c_recv, cc_s.at[0], cc_r.at[0], cdev)
    c_copy.start()
    own_s[...] = dot_t(drows[:, mine], weighted[:, half(c)], ROWS_T)
    c_copy.wait_recv()
    own_s[...] += c_recv[...].astype(jnp.float32)
    r_send[...] = own_s[...].astype(jnp.bfloat16)

    def peer8(k):
        return lax.rem(me8 + k, PEERS)

    rs = []
    for k in range(1, PEERS):
        to = peer8(k)
        cp = remote(r_send.at[pl.ds(pl.multiple_of(to * piece, 16), piece), :], r_recv.at[k - 1],
                    rs_s.at[k - 1], rs_r.at[k - 1], (to * 2 + c, x))
        cp.start()
        rs.append(cp)

    pass_z(1)
    donor_terms(1)
    accept_terms(1, w_cols)
    finish_slope(1)
    pass_y(1)
    for cp in loads[7:9]:
        cp.wait()
    spread = jnp.where(
        lax.broadcasted_iota(jnp.int32, (slab, tok), 0) // 2
        == lax.broadcasted_iota(jnp.int32, (slab, tok), 1), 0.5, 0.0)
    zeros = jnp.zeros((8, hc), jnp.float32)
    for s in range(2):
        scatter = jnp.concatenate([hot_a[s], hot_d[s], spread], axis=1).astype(jnp.bfloat16)
        grad = dot(scatter, zbuf[s]) * slope_s[s]
        grad = grad.astype(jnp.bfloat16).astype(jnp.float32)
        pad_s[s, 8 : 8 + slab, :] = grad
        head, tail = grad[0:8], grad[slab - 8 : slab]
        own_first = first if s == 0 else jnp.logical_not(first)
        pad_s[1 - s, 0:8, :] = jnp.where(own_first, tail, zeros)
        pad_s[1 - s, 8 + slab :, :] = jnp.where(own_first, zeros, head)

    pass_z(2)
    for cp in rs:
        cp.wait_recv()
    total = own_s[pl.ds(pl.multiple_of(me8 * piece, 8), piece), :]
    for k in range(PEERS - 1):
        total = total + r_recv[k].astype(jnp.float32)
    r_done[...] = total.astype(jnp.bfloat16)

    def fblock(xx, index, count=1):
        return final.at[pl.ds(pl.multiple_of(xx * hc + index * piece, 16), count * piece), half(c)]

    place = pltpu.make_async_copy(r_done, fblock(x, me8), in_sem.at[10])
    place.start()
    ag = []
    for k in range(1, PEERS):
        cp = remote(r_done, fblock(x, me8), ag_s.at[k - 1], ag_r.at[k - 1], (peer8(k) * 2 + c, x))
        cp.start()
        ag.append(cp)
    xf = [remote(r_done, fblock(x, me8), xf_s.at[0], xf_r.at[0], xdev)]
    xf[0].start()

    pass_y(2)
    pass_y(3)
    loads[9].wait()
    for hop in [None] + hops:
        def arrived(hop=hop):
            for kind in range(2):
                core_copy(kind, hop, True).wait_recv()
        when(hop, arrived)

    shift = taps // 2

    def conv(s):
        acc = None
        for tap in range(taps):
            window = pad_s[s, 8 + shift - tap : 8 + shift - tap + slab, :].astype(jnp.bfloat16)
            term = dot_t(window, wbuf[tap], COLS_T)
            acc = term if acc is None else acc + term
        return acc

    o_send[...] = conv(1).astype(jnp.bfloat16)
    o_copy = remote(o_send, o_recv, xs_s.at[1 + CHUNKS], xs_r.at[1 + CHUNKS], xdev)
    o_copy.start()

    for k in range(1, PEERS):
        ag[k - 1].wait_recv()
        part = fblock(x, lax.rem(me8 + PEERS - k, PEERS))
        cp = remote(part, part, xf_s.at[k], xf_r.at[k], xdev)
        cp.start()
        xf.append(cp)
    place.wait()
    quarter = fblock(x, 0, PEERS)
    cq = remote(quarter, quarter, cc_s.at[1], cc_r.at[1], cdev)
    cq.start()
    acc = conv(0)
    o_copy.wait_recv()
    out_ref[0] = (acc + o_recv[...].astype(jnp.float32)).astype(jnp.bfloat16)
    for cp in xf:
        cp.wait_recv()
    other = fblock(ox, 0, PEERS)
    cq2 = remote(other, other, cc_s.at[2], cc_r.at[2], cdev)
    cq2.start()
    cq.wait_recv()
    cq2.wait_recv()
    scale = 1.0 / math.sqrt(NZ * NY * NC * 2 * 2 * slots)
    pair_ref[...] = final[...].astype(jnp.float32) * scale
    for hop in [None] + hops:
        def sent(hop=hop):
            y_copy(hop).wait_send()
            for kind in range(2):
                core_copy(kind, hop).wait_send()
        when(hop, sent)
    for d in range(2):
        for s in range(NZ - 1):
            leaves = (z < NZ - 1) & (z >= s) if d == 0 else (z > 0) & (z + s < NZ)
            @pl.when(leaves)
            def _(d=d, s=s):
                z_copy(d, s).wait_send()
    for cp in [idx_copy, c_copy, cq, cq2, o_copy] + pre_copies + rs + ag + xf:
        cp.wait_send()


def per_device_kernel(pre_act, trunk_grad, conv_weight, pair_weight, donor_slots, accept_slots, junction_grad, pair_counts):
    slab, chan = pre_act.shape[1:]
    slots = donor_slots.shape[3]
    taps = conv_weight.shape[0]
    hc = chan // 2
    piece = hc // PEERS
    bf, f32 = jnp.bfloat16, jnp.float32
    V = pltpu.VMEM
    D = pltpu.SemaphoreType.DMA
    scratch = [
        V((2, slab, chan), bf), V((chan, hc), bf), V((hc, chan), bf), V(donor_slots.shape, jnp.int32),
        V(accept_slots.shape, jnp.int32), V(junction_grad.shape, f32), V(pair_counts.shape, jnp.int32),
        D((11,)),
        V((2, slab, chan), bf), V((2, slab, hc), f32), V((8, slots), f32), V((8, slots), f32),
        V((4 * slots, chan), bf), V((4 * slots, chan), bf), V((2, 4 * slots + slab // 2, hc), bf),
        V((2, slab + 16, hc), f32), V((taps, chan, hc), bf),
        V((hc, hc), bf), V((hc, hc), bf), V((hc, hc), f32), V((hc, hc), bf),
        V((PEERS - 1, piece, hc), bf), V((piece, hc), bf), V((chan, chan), bf),
        V((slab, chan), bf), V((slab, chan), bf),
        D((6,)), D((6,)), D((7,)), D((7,)), D((14,)), D((14,)),
        D((2 + CHUNKS,)), D((2 + CHUNKS,)), D((3,)), D((3,)),
        D((PEERS - 1,)), D((PEERS - 1,)), D((PEERS - 1,)), D((PEERS - 1,)), D((PEERS,)), D((PEERS,)),
        pltpu.SemaphoreType.REGULAR((6,)),
    ]
    return pl.pallas_call(
        kernel,
        out_shape=(jax.ShapeDtypeStruct(pre_act.shape, bf), jax.ShapeDtypeStruct((chan, chan), f32)),
        in_specs=[pl.BlockSpec(memory_space=pltpu.HBM)] * 8,
        out_specs=[pl.BlockSpec(memory_space=pltpu.VMEM)] * 2,
        scratch_shapes=scratch,
        compiler_params=pltpu.CompilerParams(
            collective_id=0, has_side_effects=True, vmem_limit_bytes=40 << 20),
    )(*[
        pltpu.with_memory_space_constraint(a, pltpu.HBM)
        for a in (pre_act, trunk_grad, conv_weight, pair_weight, donor_slots, accept_slots,
                  junction_grad, pair_counts)
    ])


def solution(mesh):
    in_specs = (
        P("dp", "seq", None),
        P("dp", None, "seq"),
        P(None, "dp", None),
        P(),
        P("dp", "seq", None, None),
        P("dp", "seq", None, None),
        P("dp", "seq", None, None),
        P("dp", None, None),
    )
    out_specs = (P("dp", "seq", None), P())
    fits = mesh.shape["dp"] == NZ * NY * NC and mesh.shape["seq"] == 2
    return jax.shard_map(
        per_device_kernel if fits else per_device_general, mesh=mesh, in_specs=in_specs, out_specs=out_specs, check_vma=False
    )
```

```python
import math

import jax
import jax.numpy as jnp
from jax import lax
from jax.experimental import pallas as pl
from jax.experimental.pallas import tpu as pltpu
from jax.sharding import PartitionSpec as P


def with_halo(x, sides, width):
    for axis, dim in sides:
        size, length = (lax.axis_size(axis), x.shape[dim])
        up = [(i, (i + 1) % size) for i in range(size - 1)]
        down = [(j, i) for i, j in up]
        last = lax.slice_in_dim(x, length - width, length, axis=dim)
        first = lax.slice_in_dim(x, 0, width, axis=dim)
        before = lax.ppermute(last, axis, up)
        after = lax.ppermute(first, axis, down)
        x = jnp.concatenate([before, x, after], axis=dim)
    return x


def gelu_parts(values):
    normal_cdf = 0.5 * (1.0 + jax.scipy.special.erf(values / math.sqrt(2.0)))
    density = jnp.exp(-0.5 * values * values) / math.sqrt(2.0 * math.pi)
    return (values * normal_cdf, normal_cdf + values * density)


def per_device_general(
    pre_act,
    trunk_grad,
    conv_weight,
    pair_weight,
    donor_slots,
    accept_slots,
    junction_grad,
    pair_counts,
):
    seq_count = lax.axis_size("seq")
    my_slab = lax.axis_index("seq")
    slab_len = pre_act.shape[1]
    channels = pre_act.shape[2]
    slot_count = donor_slots.shape[3]
    kernel = conv_weight.shape[0]
    half = kernel // 2
    act_f, slope = gelu_parts(pre_act[0].astype(jnp.float32))
    act = act_f.astype(jnp.bfloat16)
    arrived = lax.all_to_all(trunk_grad, "seq", split_axis=1, concat_axis=2, tiled=True)
    pooled = jnp.repeat(arrived[0].astype(jnp.float32) * 0.5, 2, axis=0)
    send_index = donor_slots[0, 0].reshape(-1)
    outgoing = act[send_index].reshape(seq_count, slot_count, channels)
    incoming = lax.all_to_all(outgoing, "seq", split_axis=0, concat_axis=0, tiled=True)
    donor_rows = incoming.reshape(-1, channels)
    accept_index = accept_slots[0, 0].reshape(-1)
    counts_in = lax.dynamic_index_in_dim(pair_counts[0], my_slab, axis=1, keepdims=False)
    live = jnp.arange(slot_count, dtype=jnp.int32)[None, :] < counts_in[:, None]
    slot_w = jnp.where(live, junction_grad[0, 0], 0.0).reshape(-1)
    accept_rows = act[accept_index]
    weighted = (slot_w[:, None] * accept_rows.astype(jnp.float32)).astype(jnp.bfloat16)
    accept_term = (
        jnp.dot(donor_rows, pair_weight, preferred_element_type=jnp.float32) * slot_w[:, None]
    )
    donor_term = lax.dot_general(
        weighted, pair_weight, (((1,), (1,)), ((), ())), preferred_element_type=jnp.float32
    ).astype(jnp.bfloat16)
    pair_part = lax.dot_general(
        donor_rows, weighted, (((0,), (0,)), ((), ())), preferred_element_type=jnp.float32
    )
    returned = lax.all_to_all(
        donor_term.reshape(seq_count, slot_count, channels),
        "seq",
        split_axis=0,
        concat_axis=0,
        tiled=True,
    )
    act_grad = (
        pooled.at[accept_index]
        .add(accept_term)
        .at[send_index]
        .add(returned.reshape(-1, channels).astype(jnp.float32))
    )
    conv_grad = (act_grad * slope).astype(jnp.bfloat16)
    padded = with_halo(conv_grad[None], (("seq", 1),), half)[0]
    piece = lax.all_gather(conv_weight, "dp", axis=1, tiled=True)
    total = jnp.zeros((slab_len, piece.shape[1]), jnp.float32)
    for tap in range(kernel):
        window = padded[2 * half - tap : 2 * half - tap + slab_len]
        total = total + lax.dot_general(
            window, piece[tap], (((1,), (1,)), ((), ())), preferred_element_type=jnp.float32
        )
    input_grad = total.astype(jnp.bfloat16)
    pair_sum = lax.psum(pair_part, ("dp", "seq"))
    scale = 1.0 / math.sqrt(lax.axis_size("dp") * seq_count * seq_count * slot_count)
    return (input_grad[None], pair_sum * scale)


MESH = pl.DeviceIdType.MESH
NZ, NY, NC = 4, 2, 2
PEERS = NZ * NY
CHUNKS = 4
TAP_PARTS = ((0, 3), (3, 2))
ROWS_T = (((0,), (0,)), ((), ()))
COLS_T = (((1,), (1,)), ((), ()))


def dot(a, b):
    return jnp.dot(a, b, preferred_element_type=jnp.float32)


def dot_t(a, b, dims):
    return lax.dot_general(a, b, dims, preferred_element_type=jnp.float32)


def kernel(
    pre_hbm, trunk_hbm, w_ref, p_hbm, ds_hbm, as_hbm, jg_hbm, pc_hbm,
    out_ref, pair_ref,
    pre_s, p_s, ds_s, as_s, jg_s, pc_s, in_sem,
    act_s, slope_s, idx_send, idx_recv, drows, weighted, zbuf, pad_s, wbuf,
    c_send, c_recv, own_s, r_send, r_recv, r_done, final, o_send, o_cat, perm_s,
    wz_s, wz_r, wy_s, wy_r, wc_s, wc_r, xs_s, xs_r, cc_s, cc_r,
    rs_s, rs_r, ag_s, ag_r, xf_s, xf_r, ready,
):
    dp = lax.axis_index("dp")
    x = lax.axis_index("seq")
    c = dp % 2
    y = (dp // 2) % 2
    z = dp // 4
    me8 = dp // 2
    ox = 1 - x
    oc = 1 - c
    slab, chan = pre_s.shape[1:]
    slots = ds_s.shape[-1]
    taps, shard = w_ref.shape[:2]
    hc = chan // 2
    tok = slab // 2
    piece = hc // PEERS
    first = x == 0

    def half(index):
        return pl.ds(pl.multiple_of(index * hc, 128), hc)

    mine, theirs = half(x), half(ox)

    def dev(zz, yy, cc):
        return (zz * NY + yy) * NC + cc

    xdev = (dp, ox)
    cdev = (me8 * 2 + oc, x)
    ydev = (dev(z, 1 - y, c), x)

    def zdev(d):
        return (dev(z + 1 if d == 0 else z - 1, y, c), x)

    def has_next(d):
        return z < NZ - 1 if d == 0 else z > 0

    relays = c == x

    def wpart(zz, yy, part):
        start, count = TAP_PARTS[part]
        return wbuf.at[pl.ds(start, count), pl.ds(pl.multiple_of((zz * NY + yy) * shard, 16), shard), :]

    def w_own(part):
        start, count = TAP_PARTS[part]
        return w_ref.at[pl.ds(start, count)]

    own_w = pltpu.make_async_copy(
        w_ref, wbuf.at[:, pl.ds(pl.multiple_of(me8 * shard, 16), shard), :], in_sem.at[8])

    def tokens(s):
        return trunk_hbm.at[0, pl.ds(pl.multiple_of((ox if s else x) * tok, 16), tok), :]

    loads = [
        pltpu.make_async_copy(src, dst, in_sem.at[i])
        for i, (src, dst) in enumerate([
            (ds_hbm, ds_s), (as_hbm, as_s), (jg_hbm, jg_s), (pc_hbm, pc_s),
            (pre_hbm.at[0], pre_s.at[0]),
            (p_hbm, p_s),
            (tokens(0), zbuf.at[0, 4 * slots :, mine]), (tokens(1), zbuf.at[1, 4 * slots :, mine])])
    ]
    for cp in loads:
        cp.start()

    @pl.when(relays)
    def _():
        own_w.start()

    barrier = pltpu.get_barrier_semaphore()
    for target in (xdev, cdev, ydev):
        pl.semaphore_signal(barrier, inc=1, device_id=target, device_id_type=MESH)
    for d in range(2):
        @pl.when(has_next(d))
        def _(d=d):
            pl.semaphore_signal(barrier, inc=1, device_id=zdev(d), device_id_type=MESH)

    def remote(src, dst, ss, rs, target):
        return pltpu.make_async_remote_copy(
            src_ref=src, dst_ref=dst, send_sem=ss, recv_sem=rs,
            device_id=target, device_id_type=MESH,
        )

    for cp in loads[:4]:
        cp.wait()

    def ordered(rows):
        a, b = rows[0:1], rows[1:2]
        return [jnp.where(first, a, b), jnp.where(first, b, a)]

    d_own = ordered(ds_s[0, 0].astype(jnp.float32))
    a_own = ordered(as_s[0, 0].astype(jnp.float32))
    counts = pc_s[0]
    cnt = jnp.where(first, counts[:, 0:1], counts[:, 1:2])
    live = lax.broadcasted_iota(jnp.int32, (2, slots), 1) < cnt
    jw_own = ordered(jnp.where(live, jg_s[0, 0], 0.0))
    nothing = jnp.zeros((2, slots), jnp.float32)
    idx_send[...] = jnp.concatenate(d_own + a_own + jw_own + [nothing], axis=0)

    edge = jnp.where((z == 0) | (z == NZ - 1), 4, 5)
    pl.semaphore_wait(barrier, edge)

    idx_copy = remote(idx_send, idx_recv, xs_s.at[0], xs_r.at[0], xdev)
    idx_copy.start()
    rows_c = slab // CHUNKS
    pre_copies = [
        remote(pre_hbm.at[0, k * rows_c : (k + 1) * rows_c, :],
               pre_s.at[1, k * rows_c : (k + 1) * rows_c, :], xs_s.at[1 + k], xs_r.at[1 + k], xdev)
        for k in range(CHUNKS)]
    trunk_copies = [
        remote(tokens(1 - s), zbuf.at[s, 4 * slots :, mine],
               xs_s.at[2 + CHUNKS + s], xs_r.at[2 + CHUNKS + s], xdev)
        for s in range(2)]
    for cp in pre_copies + trunk_copies:
        cp.start()

    hops = [(d, s) for s in range(NZ - 1) for d in range(2)]

    def entry(hop):
        return 0 if hop is None else 1 + hop[0] * 3 + hop[1]

    def source_z(hop):
        if hop is None:
            return z
        return z - 1 - hop[1] if hop[0] == 0 else z + 1 + hop[1]

    def when(hop, body):
        if hop is None:
            pl.when(relays)(body)
        else:
            pl.when(relays & (source_z(hop) >= 0 if hop[0] == 0 else source_z(hop) < NZ))(body)

    def z_copy(d, s, part):
        block = wpart(z - s if d == 0 else z + s, y, part)
        sem = 2 * (d * 3 + s) + part
        return remote(block if s else w_own(part), block, wz_s.at[sem], wz_r.at[sem], zdev(d))

    def z_arrival(d, s, part):
        block = wpart(source_z((d, s)), y, part)
        sem = 2 * (d * 3 + s) + part
        return remote(block, block, wz_s.at[sem], wz_r.at[sem], ydev)

    def y_copy(hop, part, arriving=False):
        block = wpart(source_z(hop), 1 - y if arriving else y, part)
        src = w_own(part) if hop is None and not arriving else block
        sem = 2 * entry(hop) + part
        return remote(src, block, wy_s.at[sem], wy_r.at[sem], ydev)

    def core_copy(kind, hop, part):
        block = wpart(source_z(hop), 1 - y if kind else y, part)
        src = w_own(part) if kind == 0 and hop is None else block
        sem = 2 * (kind * 7 + entry(hop)) + part
        return remote(src, block, wc_s.at[sem], wc_r.at[sem], cdev)

    for part in range(2):
        for d in range(2):
            @pl.when(relays & has_next(d))
            def _(d=d, part=part):
                z_copy(d, 0, part).start()

        @pl.when(relays)
        def _(part=part):
            y_copy(None, part).start()
            core_copy(0, None, part).start()

    def say(stage):
        for d in range(2):
            @pl.when(has_next(d))
            def _(d=d):
                pl.semaphore_signal(
                    ready.at[stage * 2 + d], inc=1, device_id=zdev(d), device_id_type=MESH)

    def hear(stage):
        for d in range(2):
            @pl.when(has_next(1 - d))
            def _(d=d):
                pl.semaphore_wait(ready.at[stage * 2 + d], 1)

    say(0)

    def pass_z(s, part):
        for d in range(2):
            def body(d=d):
                z_arrival(d, s, part).wait_recv()
                if s < NZ - 2:
                    @pl.when(has_next(d))
                    def _():
                        z_copy(d, s + 1, part).start()
                y_copy((d, s), part).start()
                core_copy(0, (d, s), part).start()
            when((d, s), body)

    def pass_y(step, part):
        for hop in [None] if step == 0 else [(0, step - 1), (1, step - 1)]:
            def body(hop=hop):
                y_copy(hop, part, True).wait_recv()
                core_copy(1, hop, part).start()
            when(hop, body)

    def gelu(s, start, count):
        rows = slice(start, start + count)
        values = pre_s[s, rows, :].astype(jnp.float32)
        normal_cdf = 0.5 * (1.0 + lax.erf(values / math.sqrt(2.0)))
        act_s[s, rows, :] = (values * normal_cdf).astype(jnp.bfloat16)
        slope_s[s, rows, :] = normal_cdf

    def finish_slope(s):
        values = pre_s[s].astype(jnp.float32)
        density = jnp.exp(-0.5 * values * values) / math.sqrt(2.0 * math.pi)
        slope_s[s] += values * density

    position = lax.broadcasted_iota(jnp.int32, (slab, 2 * slots), 0).astype(jnp.float32)

    def onehot(pair):
        return jnp.where(position == jnp.concatenate(pair, axis=1), 1.0, 0.0)

    def flip(m):
        return jnp.transpose(m).astype(jnp.bfloat16)

    def column(row):
        return jnp.transpose(jnp.broadcast_to(row, (slots, slots)))[:, 0:1]

    def block(q, r):
        return slice((2 * q + r) * slots, (2 * q + r + 1) * slots)

    def gather_donors(s, hot):
        rows = dot(flip(hot), act_s[s]).astype(jnp.bfloat16)
        for q in range(2):
            drows[block(q, s), :] = rows[q * slots : (q + 1) * slots]

    def gather_acceptors(s, hot, cols):
        rows = dot(flip(hot), act_s[s])
        for r in range(2):
            weighted[block(s, r), :] = (
                cols[r] * rows[r * slots : (r + 1) * slots]).astype(jnp.bfloat16)

    def donor_terms(q):
        term = dot_t(weighted[2 * q * slots : 2 * (q + 1) * slots, :], p_s[...], COLS_T)
        for r in range(2):
            zbuf[r, (2 + q) * slots : (3 + q) * slots, :] = (
                term[r * slots : (r + 1) * slots].astype(jnp.bfloat16))

    def accept_terms(r, cols):
        for q in range(2):
            term = dot(drows[block(q, r), :], p_s[...]) * cols[q][r]
            zbuf[q, r * slots : (r + 1) * slots, :] = term.astype(jnp.bfloat16)

    loads[4].wait()
    gelu(0, 0, slab)
    hot_d = [onehot(d_own)]
    hot_a = [onehot(a_own)]
    w_cols = [[column(w) for w in jw_own]]
    gather_donors(0, hot_d[0])
    gather_acceptors(0, hot_a[0], w_cols[0])
    hear(0)
    say(1)
    loads[5].wait()
    donor_terms(0)

    idx_copy.wait_recv()
    got = idx_recv[...]
    hot_d.append(onehot([got[1:2], got[0:1]]))
    hot_a.append(onehot([got[3:4], got[2:3]]))
    w_cols.append([column(got[5:6]), column(got[4:5])])
    accept_terms(0, w_cols)
    finish_slope(0)
    hear(1)
    say(2)
    def take(k):
        pre_copies[k].wait_recv()
        gelu(1, k * rows_c, rows_c)

    take(0)
    pass_z(0, 0)
    pass_z(0, 1)
    take(1)
    pass_z(1, 0)
    hear(2)
    take(2)
    pass_z(1, 1)
    take(3)
    gather_acceptors(1, hot_a[1], w_cols[1])
    gather_donors(1, hot_d[1])
    c_send[...] = dot_t(drows[:, mine], weighted[:, half(oc)], ROWS_T).astype(jnp.bfloat16)
    c_copy = remote(c_send, c_recv, cc_s.at[0], cc_r.at[0], cdev)
    c_copy.start()
    own_s[...] = dot_t(drows[:, mine], weighted[:, half(c)], ROWS_T)
    c_copy.wait_recv()
    own_s[...] += c_recv[...].astype(jnp.float32)
    r_send[...] = own_s[...].astype(jnp.bfloat16)

    def peer8(k):
        return lax.rem(me8 + k, PEERS)

    rs = []
    for k in range(1, PEERS):
        to = peer8(k)
        cp = remote(r_send.at[pl.ds(pl.multiple_of(to * piece, 16), piece), :], r_recv.at[k - 1],
                    rs_s.at[k - 1], rs_r.at[k - 1], (to * 2 + c, x))
        cp.start()
        rs.append(cp)

    pass_z(2, 0)
    pass_y(0, 0)
    pass_y(0, 1)
    donor_terms(1)
    accept_terms(1, w_cols)
    finish_slope(1)
    pass_z(2, 1)
    pass_y(1, 0)
    pass_y(1, 1)
    for cp in loads[6:8]:
        cp.wait()
    for cp in trunk_copies:
        cp.wait_recv()
    spread = jnp.where(
        lax.broadcasted_iota(jnp.int32, (slab, tok), 0) // 2
        == lax.broadcasted_iota(jnp.int32, (slab, tok), 1), 0.5, 0.0)
    zeros = jnp.zeros((8, chan), jnp.float32)
    for s in range(2):
        scatter = jnp.concatenate([hot_a[s], hot_d[s], spread], axis=1).astype(jnp.bfloat16)
        grad = dot(scatter, zbuf[s]) * slope_s[s]
        grad = grad.astype(jnp.bfloat16).astype(jnp.float32)
        pad_s[s, 8 : 8 + slab, :] = grad
        head, tail = grad[0:8], grad[slab - 8 : slab]
        own_first = first if s == 0 else jnp.logical_not(first)
        pad_s[1 - s, 0:8, :] = jnp.where(own_first, tail, zeros)
        pad_s[1 - s, 8 + slab :, :] = jnp.where(own_first, zeros, head)

    target = lax.broadcasted_iota(jnp.int32, (chan, 1), 0)
    part_of, rest = target // hc, target % hc
    target = rest // shard * (NC * shard) + part_of * shard + rest % shard
    perm_s[...] = jnp.where(
        lax.broadcasted_iota(jnp.int32, (chan, chan), 1) == target, 1.0, 0.0).astype(jnp.bfloat16)
    pass_y(2, 0)
    pass_y(2, 1)
    for cp in rs:
        cp.wait_recv()
    total = own_s[pl.ds(pl.multiple_of(me8 * piece, 8), piece), :]
    for k in range(PEERS - 1):
        total = total + r_recv[k].astype(jnp.float32)
    r_done[...] = total.astype(jnp.bfloat16)

    def fblock(xx, index, count=1):
        return final.at[pl.ds(pl.multiple_of(xx * hc + index * piece, 16), count * piece), half(c)]

    place = pltpu.make_async_copy(r_done, fblock(x, me8), in_sem.at[9])
    place.start()
    ag = []
    for k in range(1, PEERS):
        cp = remote(r_done, fblock(x, me8), ag_s.at[k - 1], ag_r.at[k - 1], (peer8(k) * 2 + c, x))
        cp.start()
        ag.append(cp)
    xf = [remote(r_done, fblock(x, me8), xf_s.at[0], xf_r.at[0], xdev)]
    xf[0].start()

    pass_y(3, 0)
    pass_y(3, 1)

    @pl.when(relays)
    def _():
        own_w.wait()

    def both_parts(hop, body):
        ok = (z >= 0) if hop is None else source_z(hop) >= 0 if hop[0] == 0 else source_z(hop) < NZ

        def run():
            for part in range(2):
                for kind in range(2):
                    body(core_copy(kind, hop, part))
        pl.when(jnp.logical_not(relays) & ok)(run)

    for hop in [None] + hops:
        both_parts(hop, lambda cp: cp.wait_recv())

    shift = taps // 2

    def conv(s):
        acc = None
        for tap in range(taps):
            window = pad_s[s, 8 + shift - tap : 8 + shift - tap + slab, :].astype(jnp.bfloat16)
            term = dot_t(window, wbuf[tap], COLS_T)
            acc = term if acc is None else acc + term
        return acc

    o_send[...] = conv(1).astype(jnp.bfloat16)
    o_copy = remote(o_send, o_cat.at[:, mine], xs_s.at[1 + CHUNKS], xs_r.at[1 + CHUNKS], xdev)
    o_copy.start()

    for k in range(1, PEERS):
        ag[k - 1].wait_recv()
        part = fblock(x, lax.rem(me8 + PEERS - k, PEERS))
        cp = remote(part, part, xf_s.at[k], xf_r.at[k], xdev)
        cp.start()
        xf.append(cp)
    place.wait()
    quarter = fblock(x, 0, PEERS)
    cq = remote(quarter, quarter, cc_s.at[1], cc_r.at[1], cdev)
    cq.start()
    o_cat[:, mine] = conv(0).astype(jnp.bfloat16)
    o_copy.wait_recv()
    out_ref[0] = dot(o_cat[...], perm_s[...]).astype(jnp.bfloat16)
    for cp in xf:
        cp.wait_recv()
    other = fblock(ox, 0, PEERS)
    cq2 = remote(other, other, cc_s.at[2], cc_r.at[2], cdev)
    cq2.start()
    cq.wait_recv()
    cq2.wait_recv()
    scale = 1.0 / math.sqrt(NZ * NY * NC * 2 * 2 * slots)
    pair_ref[...] = final[...].astype(jnp.float32) * scale
    for hop in [None] + hops:
        def sent(hop=hop):
            for part in range(2):
                y_copy(hop, part).wait_send()
                for kind in range(2):
                    core_copy(kind, hop, part).wait_send()
        when(hop, sent)
    for d in range(2):
        for s in range(NZ - 1):
            leaves = (z < NZ - 1) & (z >= s) if d == 0 else (z > 0) & (z + s < NZ)
            @pl.when(relays & leaves)
            def _(d=d, s=s):
                for part in range(2):
                    z_copy(d, s, part).wait_send()
    for cp in [idx_copy, c_copy, cq, cq2, o_copy] + pre_copies + trunk_copies + rs + ag + xf:
        cp.wait_send()


def per_device_kernel(pre_act, trunk_grad, conv_weight, pair_weight, donor_slots, accept_slots, junction_grad, pair_counts):
    slab, chan = pre_act.shape[1:]
    slots = donor_slots.shape[3]
    taps = conv_weight.shape[0]
    hc = chan // 2
    piece = hc // PEERS
    bf, f32 = jnp.bfloat16, jnp.float32
    V = pltpu.VMEM
    D = pltpu.SemaphoreType.DMA
    scratch = [
        V((2, slab, chan), bf), V((chan, chan), bf), V(donor_slots.shape, jnp.int32),
        V(accept_slots.shape, jnp.int32), V(junction_grad.shape, f32), V(pair_counts.shape, jnp.int32),
        D((10,)),
        V((2, slab, chan), bf), V((2, slab, chan), f32), V((8, slots), f32), V((8, slots), f32),
        V((4 * slots, chan), bf), V((4 * slots, chan), bf), V((2, 4 * slots + slab // 2, chan), bf),
        V((2, slab + 16, chan), f32), V((taps, hc, chan), bf),
        V((hc, hc), bf), V((hc, hc), bf), V((hc, hc), f32), V((hc, hc), bf),
        V((PEERS - 1, piece, hc), bf), V((piece, hc), bf), V((chan, chan), bf),
        V((slab, hc), bf), V((slab, chan), bf), V((chan, chan), bf),
        D((12,)), D((12,)), D((14,)), D((14,)), D((28,)), D((28,)),
        D((4 + CHUNKS,)), D((4 + CHUNKS,)), D((3,)), D((3,)),
        D((PEERS - 1,)), D((PEERS - 1,)), D((PEERS - 1,)), D((PEERS - 1,)), D((PEERS,)), D((PEERS,)),
        pltpu.SemaphoreType.REGULAR((6,)),
    ]
    return pl.pallas_call(
        kernel,
        out_shape=(jax.ShapeDtypeStruct(pre_act.shape, bf), jax.ShapeDtypeStruct((chan, chan), f32)),
        in_specs=[pl.BlockSpec(memory_space=pltpu.HBM)] * 8,
        out_specs=[pl.BlockSpec(memory_space=pltpu.VMEM)] * 2,
        scratch_shapes=scratch,
        compiler_params=pltpu.CompilerParams(
            collective_id=0, has_side_effects=True, vmem_limit_bytes=40 << 20),
    )(*[
        pltpu.with_memory_space_constraint(a, pltpu.HBM)
        for a in (pre_act, trunk_grad, conv_weight, pair_weight, donor_slots, accept_slots,
                  junction_grad, pair_counts)
    ])


def solution(mesh):
    in_specs = (
        P("dp", "seq", None),
        P("dp", None, "seq"),
        P(None, "dp", None),
        P(),
        P("dp", "seq", None, None),
        P("dp", "seq", None, None),
        P("dp", "seq", None, None),
        P("dp", None, None),
    )
    out_specs = (P("dp", "seq", None), P())
    fits = mesh.shape["dp"] == NZ * NY * NC and mesh.shape["seq"] == 2
    return jax.shard_map(
        per_device_kernel if fits else per_device_general, mesh=mesh, in_specs=in_specs, out_specs=out_specs, check_vma=False
    )
```

```python
import functools
import math

import jax
import jax.numpy as jnp
from jax import lax
from jax.experimental import pallas as pl
from jax.experimental.pallas import tpu as pltpu
from jax.sharding import PartitionSpec as P


def with_halo(x, sides, width):
    for axis, dim in sides:
        size, length = (lax.axis_size(axis), x.shape[dim])
        up = [(i, (i + 1) % size) for i in range(size - 1)]
        down = [(j, i) for i, j in up]
        last = lax.slice_in_dim(x, length - width, length, axis=dim)
        first = lax.slice_in_dim(x, 0, width, axis=dim)
        before = lax.ppermute(last, axis, up)
        after = lax.ppermute(first, axis, down)
        x = jnp.concatenate([before, x, after], axis=dim)
    return x


def gelu_parts(values):
    normal_cdf = 0.5 * (1.0 + jax.scipy.special.erf(values / math.sqrt(2.0)))
    density = jnp.exp(-0.5 * values * values) / math.sqrt(2.0 * math.pi)
    return (values * normal_cdf, normal_cdf + values * density)


def per_device_general(
    pre_act,
    trunk_grad,
    conv_weight,
    pair_weight,
    donor_slots,
    accept_slots,
    junction_grad,
    pair_counts,
):
    seq_count = lax.axis_size("seq")
    my_slab = lax.axis_index("seq")
    slab_len = pre_act.shape[1]
    channels = pre_act.shape[2]
    slot_count = donor_slots.shape[3]
    kernel = conv_weight.shape[0]
    half = kernel // 2
    act_f, slope = gelu_parts(pre_act[0].astype(jnp.float32))
    act = act_f.astype(jnp.bfloat16)
    arrived = lax.all_to_all(trunk_grad, "seq", split_axis=1, concat_axis=2, tiled=True)
    pooled = jnp.repeat(arrived[0].astype(jnp.float32) * 0.5, 2, axis=0)
    send_index = donor_slots[0, 0].reshape(-1)
    outgoing = act[send_index].reshape(seq_count, slot_count, channels)
    incoming = lax.all_to_all(outgoing, "seq", split_axis=0, concat_axis=0, tiled=True)
    donor_rows = incoming.reshape(-1, channels)
    accept_index = accept_slots[0, 0].reshape(-1)
    counts_in = lax.dynamic_index_in_dim(pair_counts[0], my_slab, axis=1, keepdims=False)
    live = jnp.arange(slot_count, dtype=jnp.int32)[None, :] < counts_in[:, None]
    slot_w = jnp.where(live, junction_grad[0, 0], 0.0).reshape(-1)
    accept_rows = act[accept_index]
    weighted = (slot_w[:, None] * accept_rows.astype(jnp.float32)).astype(jnp.bfloat16)
    accept_term = (
        jnp.dot(donor_rows, pair_weight, preferred_element_type=jnp.float32) * slot_w[:, None]
    )
    donor_term = lax.dot_general(
        weighted, pair_weight, (((1,), (1,)), ((), ())), preferred_element_type=jnp.float32
    ).astype(jnp.bfloat16)
    pair_part = lax.dot_general(
        donor_rows, weighted, (((0,), (0,)), ((), ())), preferred_element_type=jnp.float32
    )
    returned = lax.all_to_all(
        donor_term.reshape(seq_count, slot_count, channels),
        "seq",
        split_axis=0,
        concat_axis=0,
        tiled=True,
    )
    act_grad = (
        pooled.at[accept_index]
        .add(accept_term)
        .at[send_index]
        .add(returned.reshape(-1, channels).astype(jnp.float32))
    )
    conv_grad = (act_grad * slope).astype(jnp.bfloat16)
    padded = with_halo(conv_grad[None], (("seq", 1),), half)[0]
    piece = lax.all_gather(conv_weight, "dp", axis=1, tiled=True)
    total = jnp.zeros((slab_len, piece.shape[1]), jnp.float32)
    for tap in range(kernel):
        window = padded[2 * half - tap : 2 * half - tap + slab_len]
        total = total + lax.dot_general(
            window, piece[tap], (((1,), (1,)), ((), ())), preferred_element_type=jnp.float32
        )
    input_grad = total.astype(jnp.bfloat16)
    pair_sum = lax.psum(pair_part, ("dp", "seq"))
    scale = 1.0 / math.sqrt(lax.axis_size("dp") * seq_count * seq_count * slot_count)
    return (input_grad[None], pair_sum * scale)


MESH = pl.DeviceIdType.MESH
NZ, NY, NC = 4, 2, 2
PEERS = NZ * NY
CHUNKS = 4
FINISH_PARTS = 4
SEND_ORDER = (1, 2, 3, 4, 5, 6, 7)
TAP_PARTS = ((0, 3), (3, 2))
ROWS_T = (((0,), (0,)), ((), ()))
COLS_T = (((1,), (1,)), ((), ()))


def dot(a, b):
    return jnp.dot(a, b, preferred_element_type=jnp.float32)


def dot_t(a, b, dims):
    return lax.dot_general(a, b, dims, preferred_element_type=jnp.float32)


def kernel(
    pre_hbm, trunk_hbm, w_ref, p_hbm, ds_hbm, as_hbm, jg_hbm, pc_hbm,
    out_ref, final,
    pre_s, p_s, ds_s, as_s, jg_s, pc_s, in_sem,
    act_s, slope_s, idx_send, idx_recv, drows, weighted, zbuf, pad_s, wbuf,
    c_send, c_recv, own_s, r_send, r_recv, r_done, o_send, o_all, perm_s,
    wz_s, wz_r, wy_s, wy_r, wc_s, wc_r, xs_s, xs_r, cc_s, cc_r,
    rs_s, rs_r, ag_s, ag_r, xf_s, xf_r, ready,
):
    dp = lax.axis_index("dp")
    x = lax.axis_index("seq")
    c = dp % 2
    y = (dp // 2) % 2
    z = dp // 4
    me8 = dp // 2
    ox = 1 - x
    oc = 1 - c
    slab, chan = pre_s.shape[1:]
    slots = ds_s.shape[-1]
    taps, shard = w_ref.shape[:2]
    hc = chan // 2
    tok = slab // 2
    piece = hc // PEERS
    line = NZ * shard
    first = x == 0

    def half(index):
        return pl.ds(pl.multiple_of(index * hc, 128), hc)

    mine, theirs = half(x), half(ox)

    def dev(zz, yy, cc):
        return (zz * NY + yy) * NC + cc

    xdev = (dp, ox)
    cdev = (me8 * 2 + oc, x)
    ydev = (dev(z, 1 - y, c), x)

    def zdev(d):
        return (dev(z + 1 if d == 0 else z - 1, y, c), x)

    def has_next(d):
        return z < NZ - 1 if d == 0 else z > 0

    relays = c == x

    def wpart(zz, yy, part):
        start, count = TAP_PARTS[part]
        return wbuf.at[pl.ds(start, count), pl.ds(pl.multiple_of((yy * NZ + zz) * shard, 16), shard), :]

    def w_own(part):
        start, count = TAP_PARTS[part]
        return w_ref.at[pl.ds(start, count)]

    own_w = pltpu.make_async_copy(
        w_ref, wbuf.at[:, pl.ds(pl.multiple_of((y * NZ + z) * shard, 16), shard), :], in_sem.at[8])

    def tokens(s):
        return trunk_hbm.at[0, pl.ds(pl.multiple_of((ox if s else x) * tok, 16), tok), :]

    loads = [
        pltpu.make_async_copy(src, dst, in_sem.at[i])
        for i, (src, dst) in enumerate([
            (ds_hbm, ds_s), (as_hbm, as_s), (jg_hbm, jg_s), (pc_hbm, pc_s),
            (pre_hbm.at[0], pre_s.at[0]),
            (p_hbm, p_s),
            (tokens(0), zbuf.at[0, 4 * slots :, mine]), (tokens(1), zbuf.at[1, 4 * slots :, mine])])
    ]
    for cp in loads:
        cp.start()

    @pl.when(relays)
    def _():
        own_w.start()

    barrier = pltpu.get_barrier_semaphore()
    for target in (xdev, cdev, ydev):
        pl.semaphore_signal(barrier, inc=1, device_id=target, device_id_type=MESH)
    for d in range(2):
        @pl.when(has_next(d))
        def _(d=d):
            pl.semaphore_signal(barrier, inc=1, device_id=zdev(d), device_id_type=MESH)

    def remote(src, dst, ss, rs, target):
        return pltpu.make_async_remote_copy(
            src_ref=src, dst_ref=dst, send_sem=ss, recv_sem=rs,
            device_id=target, device_id_type=MESH,
        )

    for cp in loads[:4]:
        cp.wait()

    def ordered(rows):
        a, b = rows[0:1], rows[1:2]
        return [jnp.where(first, a, b), jnp.where(first, b, a)]

    d_own = ordered(ds_s[0, 0].astype(jnp.float32))
    a_own = ordered(as_s[0, 0].astype(jnp.float32))
    counts = pc_s[0]
    cnt = jnp.where(first, counts[:, 0:1], counts[:, 1:2])
    live = lax.broadcasted_iota(jnp.int32, (2, slots), 1) < cnt
    jw_own = ordered(jnp.where(live, jg_s[0, 0], 0.0))
    nothing = jnp.zeros((2, slots), jnp.float32)
    idx_send[...] = jnp.concatenate(d_own + a_own + jw_own + [nothing], axis=0)

    edge = jnp.where((z == 0) | (z == NZ - 1), 4, 5)
    pl.semaphore_wait(barrier, edge)

    idx_copy = remote(idx_send, idx_recv, xs_s.at[0], xs_r.at[0], xdev)
    idx_copy.start()
    rows_c = slab // CHUNKS
    pre_copies = [
        remote(pre_hbm.at[0, k * rows_c : (k + 1) * rows_c, :],
               pre_s.at[1, k * rows_c : (k + 1) * rows_c, :], xs_s.at[1 + k], xs_r.at[1 + k], xdev)
        for k in range(CHUNKS)]
    trunk_copies = [
        remote(tokens(1 - s), zbuf.at[s, 4 * slots :, mine],
               xs_s.at[2 + CHUNKS + s], xs_r.at[2 + CHUNKS + s], xdev)
        for s in range(2)]
    for cp in pre_copies:
        cp.start()

    hops = [(d, s) for s in range(NZ - 1) for d in range(2)]

    def entry(hop):
        return 0 if hop is None else 1 + hop[0] * 3 + hop[1]

    def source_z(hop):
        if hop is None:
            return z
        return z - 1 - hop[1] if hop[0] == 0 else z + 1 + hop[1]

    def when(hop, body):
        if hop is None:
            pl.when(relays)(body)
        else:
            pl.when(relays & (source_z(hop) >= 0 if hop[0] == 0 else source_z(hop) < NZ))(body)

    def z_copy(d, s, part):
        block = wpart(z - s if d == 0 else z + s, y, part)
        sem = 2 * (d * 3 + s) + part
        return remote(block if s else w_own(part), block, wz_s.at[sem], wz_r.at[sem], zdev(d))

    def z_arrival(d, s, part):
        block = wpart(source_z((d, s)), y, part)
        sem = 2 * (d * 3 + s) + part
        return remote(block, block, wz_s.at[sem], wz_r.at[sem], ydev)

    def y_copy(hop, part, arriving=False):
        block = wpart(source_z(hop), 1 - y if arriving else y, part)
        src = w_own(part) if hop is None and not arriving else block
        sem = 2 * entry(hop) + part
        return remote(src, block, wy_s.at[sem], wy_r.at[sem], ydev)

    def core_copy(kind, hop, part):
        block = wpart(source_z(hop), 1 - y if kind else y, part)
        src = w_own(part) if kind == 0 and hop is None else block
        sem = 2 * (kind * 7 + entry(hop)) + part
        return remote(src, block, wc_s.at[sem], wc_r.at[sem], cdev)

    for part in range(2):
        for d in range(2):
            @pl.when(relays & has_next(d))
            def _(d=d, part=part):
                z_copy(d, 0, part).start()

        @pl.when(relays)
        def _(part=part):
            y_copy(None, part).start()
            core_copy(0, None, part).start()

    def say(stage):
        for d in range(2):
            @pl.when(has_next(d))
            def _(d=d):
                pl.semaphore_signal(
                    ready.at[stage * 2 + d], inc=1, device_id=zdev(d), device_id_type=MESH)

    def hear(stage):
        for d in range(2):
            @pl.when(has_next(1 - d))
            def _(d=d):
                pl.semaphore_wait(ready.at[stage * 2 + d], 1)

    say(0)

    def pass_z(s, part):
        for d in range(2):
            def body(d=d):
                z_arrival(d, s, part).wait_recv()
                if s < NZ - 2:
                    @pl.when(has_next(d))
                    def _():
                        z_copy(d, s + 1, part).start()
                y_copy((d, s), part).start()
                core_copy(0, (d, s), part).start()
            when((d, s), body)

    def pass_y(step, part):
        for hop in [None] if step == 0 else [(0, step - 1), (1, step - 1)]:
            def body(hop=hop):
                y_copy(hop, part, True).wait_recv()
                core_copy(1, hop, part).start()
            when(hop, body)

    def gelu(s, start, count):
        rows = slice(start, start + count)
        values = pre_s[s, rows, :].astype(jnp.float32)
        normal_cdf = 0.5 * (1.0 + lax.erf(values / math.sqrt(2.0)))
        act_s[s, rows, :] = (values * normal_cdf).astype(jnp.bfloat16)
        slope_s[s, rows, :] = normal_cdf

    def finish_slope(s):
        values = pre_s[s].astype(jnp.float32)
        density = jnp.exp(-0.5 * values * values) / math.sqrt(2.0 * math.pi)
        slope_s[s] += values * density

    position = lax.broadcasted_iota(jnp.int32, (slab, 2 * slots), 0).astype(jnp.float32)

    def onehot(pair):
        return jnp.where(position == jnp.concatenate(pair, axis=1), 1.0, 0.0)

    def flip(m):
        return jnp.transpose(m).astype(jnp.bfloat16)

    def column(row):
        return jnp.transpose(jnp.broadcast_to(row, (slots, slots)))[:, 0:1]

    def block(q, r):
        return slice((2 * q + r) * slots, (2 * q + r + 1) * slots)

    def gather_donors(s, hot):
        rows = dot(flip(hot), act_s[s]).astype(jnp.bfloat16)
        for q in range(2):
            drows[block(q, s), :] = rows[q * slots : (q + 1) * slots]

    def gather_acceptors(s, hot, cols):
        rows = dot(flip(hot), act_s[s])
        for r in range(2):
            weighted[block(s, r), :] = (
                cols[r] * rows[r * slots : (r + 1) * slots]).astype(jnp.bfloat16)

    def donor_terms(q):
        term = dot_t(weighted[2 * q * slots : 2 * (q + 1) * slots, :], p_s[...], COLS_T)
        for r in range(2):
            zbuf[r, (2 + q) * slots : (3 + q) * slots, :] = (
                term[r * slots : (r + 1) * slots].astype(jnp.bfloat16))

    def accept_terms(r, cols):
        for q in range(2):
            term = dot(drows[block(q, r), :], p_s[...]) * cols[q][r]
            zbuf[q, r * slots : (r + 1) * slots, :] = term.astype(jnp.bfloat16)

    loads[4].wait()
    gelu(0, 0, slab)
    hot_d = [onehot(d_own)]
    hot_a = [onehot(a_own)]
    w_cols = [[column(w) for w in jw_own]]
    gather_donors(0, hot_d[0])
    gather_acceptors(0, hot_a[0], w_cols[0])
    hear(0)
    say(1)
    loads[5].wait()
    donor_terms(0)

    idx_copy.wait_recv()
    got = idx_recv[...]
    hot_d.append(onehot([got[1:2], got[0:1]]))
    hot_a.append(onehot([got[3:4], got[2:3]]))
    w_cols.append([column(got[5:6]), column(got[4:5])])
    accept_terms(0, w_cols)
    finish_slope(0)
    hear(1)
    say(2)
    def take(k):
        pre_copies[k].wait_recv()
        gelu(1, k * rows_c, rows_c)

    take(0)
    pass_z(0, 0)
    pass_z(0, 1)
    take(1)
    for cp in trunk_copies:
        cp.start()
    pass_z(1, 0)
    hear(2)
    take(2)
    pass_z(1, 1)
    take(3)
    gather_acceptors(1, hot_a[1], w_cols[1])
    gather_donors(1, hot_d[1])
    c_send[...] = dot_t(drows[:, mine], weighted[:, half(oc)], ROWS_T).astype(jnp.bfloat16)
    c_copy = remote(c_send, c_recv, cc_s.at[0], cc_r.at[0], cdev)
    c_copy.start()
    own_s[...] = dot_t(drows[:, mine], weighted[:, half(c)], ROWS_T)
    c_copy.wait_recv()
    own_s[...] += c_recv[...].astype(jnp.float32)
    r_send[...] = own_s[...].astype(jnp.bfloat16)

    def peer8(k):
        zz = [z, z + 1 - 2 * (z % 2), lax.rem(z + 2, NZ), NZ - 1 - z][k // 2]
        return zz * NY + (1 - y if k % 2 else y)

    rs = {}
    for k in SEND_ORDER:
        to = peer8(k)
        rs[k] = remote(r_send.at[pl.ds(pl.multiple_of(to * piece, 16), piece), :], r_recv.at[k - 1],
                       rs_s.at[k - 1], rs_r.at[k - 1], (to * 2 + c, x))
        rs[k].start()

    pass_z(2, 0)
    pass_y(0, 0)
    pass_y(0, 1)
    donor_terms(1)
    accept_terms(1, w_cols)
    finish_slope(1)
    pass_z(2, 1)
    pass_y(1, 0)
    pass_y(1, 1)
    for cp in loads[6:8]:
        cp.wait()
    for cp in trunk_copies:
        cp.wait_recv()
    spread = jnp.where(
        lax.broadcasted_iota(jnp.int32, (slab, tok), 0) // 2
        == lax.broadcasted_iota(jnp.int32, (slab, tok), 1), 0.5, 0.0)
    zeros = jnp.zeros((8, chan), jnp.float32)
    for s in range(2):
        scatter = jnp.concatenate([hot_a[s], hot_d[s], spread], axis=1).astype(jnp.bfloat16)
        grad = dot(scatter, zbuf[s]) * slope_s[s]
        grad = grad.astype(jnp.bfloat16).astype(jnp.float32)
        pad_s[s, 8 : 8 + slab, :] = grad
        head, tail = grad[0:8], grad[slab - 8 : slab]
        own_first = first if s == 0 else jnp.logical_not(first)
        pad_s[1 - s, 0:8, :] = jnp.where(own_first, tail, zeros)
        pad_s[1 - s, 8 + slab :, :] = jnp.where(own_first, zeros, head)

    @pl.when(relays)
    def _():
        own_w.wait()

    def lines_in(kind):
        for hop in [None] + hops:
            ok = (z >= 0) if hop is None else source_z(hop) >= 0 if hop[0] == 0 else source_z(hop) < NZ

            def run(hop=hop):
                for part in range(2):
                    core_copy(kind, hop, part).wait_recv()
            pl.when(jnp.logical_not(relays) & ok)(run)

    shift = taps // 2

    def conv(s, yy):
        acc = None
        for tap in range(taps):
            window = pad_s[s, 8 + shift - tap : 8 + shift - tap + slab, :].astype(jnp.bfloat16)
            term = dot_t(window, wbuf[tap, pl.ds(pl.multiple_of(yy * line, 16), line), :], COLS_T)
            acc = term if acc is None else acc + term
        return acc.astype(jnp.bfloat16)

    def give(kind):
        yy = 1 - y if kind else y
        o_send[kind] = conv(1, yy)
        cp = remote(o_send.at[kind], o_all.at[2 * x + yy],
                    xs_s.at[4 + CHUNKS + kind], xs_r.at[4 + CHUNKS + kind], xdev)
        cp.start()
        return cp

    lines_in(0)
    o_copies = [give(0)]
    target = lax.broadcasted_iota(jnp.int32, (chan, 1), 0)
    part_of, target = target // hc, target % hc
    line_of, target = target // line, target % line
    target = (target // shard * NY + line_of) * (NC * shard) + part_of * shard + target % shard
    perm_s[...] = jnp.where(
        lax.broadcasted_iota(jnp.int32, (chan, chan), 1) == target, 1.0, 0.0).astype(jnp.bfloat16)
    pass_y(2, 0)
    pass_y(2, 1)
    for k in range(1, PEERS):
        rs[k].wait_recv()
    total = own_s[pl.ds(pl.multiple_of(me8 * piece, 8), piece), :]
    for k in range(PEERS - 1):
        total = total + r_recv[k].astype(jnp.float32)
    r_done[...] = total.astype(jnp.bfloat16)

    def fblock(xx, index, count=1):
        return final.at[pl.ds(pl.multiple_of(xx * hc + index * piece, 16), count * piece), half(c)]

    place = pltpu.make_async_copy(r_done, fblock(x, me8), in_sem.at[9])
    place.start()
    ag = {}
    for k in SEND_ORDER:
        ag[k] = remote(r_done, fblock(x, me8), ag_s.at[k - 1], ag_r.at[k - 1], (peer8(k) * 2 + c, x))
        ag[k].start()
    xf = [remote(r_done, fblock(x, me8), xf_s.at[0], xf_r.at[0], xdev)]
    xf[0].start()

    pass_y(3, 0)
    pass_y(3, 1)
    lines_in(1)
    o_copies.append(give(1))
    for k in range(1, PEERS):
        ag[k].wait_recv()
        part = fblock(x, peer8(k))
        cp = remote(part, part, xf_s.at[k], xf_r.at[k], xdev)
        cp.start()
        xf.append(cp)
    place.wait()
    quarter = fblock(x, 0, PEERS)
    cq = remote(quarter, quarter, cc_s.at[1], cc_r.at[1], cdev)
    cq.start()
    for yy in range(NY):
        o_all[2 * x + yy] = conv(0, yy)
    for cp in o_copies:
        cp.wait_recv()
    out_ref[0] = sum(
        dot(o_all[k], perm_s[k * line : (k + 1) * line, :]) for k in range(2 * NY)
    ).astype(jnp.bfloat16)
    for cp in xf:
        cp.wait_recv()
    other = fblock(ox, 0, PEERS)
    cq2 = remote(other, other, cc_s.at[2], cc_r.at[2], cdev)
    cq2.start()
    cq.wait_recv()
    cq2.wait_recv()
    for hop in [None] + hops:
        def sent(hop=hop):
            for part in range(2):
                y_copy(hop, part).wait_send()
                for kind in range(2):
                    core_copy(kind, hop, part).wait_send()
        when(hop, sent)
    for d in range(2):
        for s in range(NZ - 1):
            leaves = (z < NZ - 1) & (z >= s) if d == 0 else (z > 0) & (z + s < NZ)
            @pl.when(relays & leaves)
            def _(d=d, s=s):
                for part in range(2):
                    z_copy(d, s, part).wait_send()
    for cp in [idx_copy, c_copy, cq, cq2] + o_copies + pre_copies + trunk_copies + list(rs.values()) + list(ag.values()) + xf:
        cp.wait_send()


def finish(scale, grad_ref, final, out_hbm, pair_hbm, scaled, sem):
    copies = [pltpu.make_async_copy(grad_ref, out_hbm, sem.at[0])]
    copies[0].start()
    rows = final.shape[0] // FINISH_PARTS
    for k in range(FINISH_PARTS):
        part = slice(k * rows, (k + 1) * rows)
        scaled[part, :] = final[part, :].astype(jnp.float32) * scale
        copies.append(pltpu.make_async_copy(scaled.at[part, :], pair_hbm.at[part, :], sem.at[k + 1]))
        copies[-1].start()
    for cp in copies:
        cp.wait()


def per_device_kernel(pre_act, trunk_grad, conv_weight, pair_weight, donor_slots, accept_slots, junction_grad, pair_counts):
    slab, chan = pre_act.shape[1:]
    slots = donor_slots.shape[3]
    taps = conv_weight.shape[0]
    hc = chan // 2
    piece = hc // PEERS
    bf, f32 = jnp.bfloat16, jnp.float32
    V = pltpu.VMEM
    D = pltpu.SemaphoreType.DMA
    scratch = [
        V((2, slab, chan), bf), V((chan, chan), bf), V(donor_slots.shape, jnp.int32),
        V(accept_slots.shape, jnp.int32), V(junction_grad.shape, f32), V(pair_counts.shape, jnp.int32),
        D((10,)),
        V((2, slab, chan), bf), V((2, slab, chan), f32), V((8, slots), f32), V((8, slots), f32),
        V((4 * slots, chan), bf), V((4 * slots, chan), bf), V((2, 4 * slots + slab // 2, chan), bf),
        V((2, slab + 16, chan), f32), V((taps, hc, chan), bf),
        V((hc, hc), bf), V((hc, hc), bf), V((hc, hc), f32), V((hc, hc), bf),
        V((PEERS - 1, piece, hc), bf), V((piece, hc), bf),
        V((NY, slab, hc // NY), bf), V((2 * NY, slab, hc // NY), bf), V((chan, chan), bf),
        D((12,)), D((12,)), D((14,)), D((14,)), D((28,)), D((28,)),
        D((6 + CHUNKS,)), D((6 + CHUNKS,)), D((3,)), D((3,)),
        D((PEERS - 1,)), D((PEERS - 1,)), D((PEERS - 1,)), D((PEERS - 1,)), D((PEERS,)), D((PEERS,)),
        pltpu.SemaphoreType.REGULAR((6,)),
    ]
    done = pl.pallas_call(
        kernel,
        out_shape=(jax.ShapeDtypeStruct(pre_act.shape, bf), jax.ShapeDtypeStruct((chan, chan), bf)),
        in_specs=[pl.BlockSpec(memory_space=pltpu.HBM)] * 8,
        out_specs=[pl.BlockSpec(memory_space=pltpu.VMEM)] * 2,
        scratch_shapes=scratch,
        compiler_params=pltpu.CompilerParams(
            collective_id=0, has_side_effects=True, vmem_limit_bytes=40 << 20),
    )(*[
        pltpu.with_memory_space_constraint(a, pltpu.HBM)
        for a in (pre_act, trunk_grad, conv_weight, pair_weight, donor_slots, accept_slots,
                  junction_grad, pair_counts)
    ])
    scale = 1.0 / math.sqrt(NZ * NY * NC * 2 * 2 * slots)
    return pl.pallas_call(
        functools.partial(finish, scale),
        out_shape=(jax.ShapeDtypeStruct(pre_act.shape, bf), jax.ShapeDtypeStruct((chan, chan), f32)),
        in_specs=[pl.BlockSpec(memory_space=pltpu.VMEM)] * 2,
        out_specs=[pl.BlockSpec(memory_space=pltpu.HBM)] * 2,
        scratch_shapes=[V((chan, chan), f32), D((FINISH_PARTS + 1,))],
    )(*[pltpu.with_memory_space_constraint(a, pltpu.VMEM) for a in done])


def solution(mesh):
    in_specs = (
        P("dp", "seq", None),
        P("dp", None, "seq"),
        P(None, "dp", None),
        P(),
        P("dp", "seq", None, None),
        P("dp", "seq", None, None),
        P("dp", "seq", None, None),
        P("dp", None, None),
    )
    out_specs = (P("dp", "seq", None), P())
    fits = mesh.shape["dp"] == NZ * NY * NC and mesh.shape["seq"] == 2
    return jax.shard_map(
        per_device_kernel if fits else per_device_general, mesh=mesh, in_specs=in_specs, out_specs=out_specs, check_vma=False
    )
```

```python
import functools
import math

import jax
import jax.numpy as jnp
from jax import lax
from jax.experimental import pallas as pl
from jax.experimental.pallas import tpu as pltpu
from jax.sharding import PartitionSpec as P


def with_halo(x, sides, width):
    for axis, dim in sides:
        size, length = (lax.axis_size(axis), x.shape[dim])
        up = [(i, (i + 1) % size) for i in range(size - 1)]
        down = [(j, i) for i, j in up]
        last = lax.slice_in_dim(x, length - width, length, axis=dim)
        first = lax.slice_in_dim(x, 0, width, axis=dim)
        before = lax.ppermute(last, axis, up)
        after = lax.ppermute(first, axis, down)
        x = jnp.concatenate([before, x, after], axis=dim)
    return x


def gelu_parts(values):
    normal_cdf = 0.5 * (1.0 + jax.scipy.special.erf(values / math.sqrt(2.0)))
    density = jnp.exp(-0.5 * values * values) / math.sqrt(2.0 * math.pi)
    return (values * normal_cdf, normal_cdf + values * density)


def per_device_general(
    pre_act,
    trunk_grad,
    conv_weight,
    pair_weight,
    donor_slots,
    accept_slots,
    junction_grad,
    pair_counts,
):
    seq_count = lax.axis_size("seq")
    my_slab = lax.axis_index("seq")
    slab_len = pre_act.shape[1]
    channels = pre_act.shape[2]
    slot_count = donor_slots.shape[3]
    kernel = conv_weight.shape[0]
    half = kernel // 2
    act_f, slope = gelu_parts(pre_act[0].astype(jnp.float32))
    act = act_f.astype(jnp.bfloat16)
    arrived = lax.all_to_all(trunk_grad, "seq", split_axis=1, concat_axis=2, tiled=True)
    pooled = jnp.repeat(arrived[0].astype(jnp.float32) * 0.5, 2, axis=0)
    send_index = donor_slots[0, 0].reshape(-1)
    outgoing = act[send_index].reshape(seq_count, slot_count, channels)
    incoming = lax.all_to_all(outgoing, "seq", split_axis=0, concat_axis=0, tiled=True)
    donor_rows = incoming.reshape(-1, channels)
    accept_index = accept_slots[0, 0].reshape(-1)
    counts_in = lax.dynamic_index_in_dim(pair_counts[0], my_slab, axis=1, keepdims=False)
    live = jnp.arange(slot_count, dtype=jnp.int32)[None, :] < counts_in[:, None]
    slot_w = jnp.where(live, junction_grad[0, 0], 0.0).reshape(-1)
    accept_rows = act[accept_index]
    weighted = (slot_w[:, None] * accept_rows.astype(jnp.float32)).astype(jnp.bfloat16)
    accept_term = (
        jnp.dot(donor_rows, pair_weight, preferred_element_type=jnp.float32) * slot_w[:, None]
    )
    donor_term = lax.dot_general(
        weighted, pair_weight, (((1,), (1,)), ((), ())), preferred_element_type=jnp.float32
    ).astype(jnp.bfloat16)
    pair_part = lax.dot_general(
        donor_rows, weighted, (((0,), (0,)), ((), ())), preferred_element_type=jnp.float32
    )
    returned = lax.all_to_all(
        donor_term.reshape(seq_count, slot_count, channels),
        "seq",
        split_axis=0,
        concat_axis=0,
        tiled=True,
    )
    act_grad = (
        pooled.at[accept_index]
        .add(accept_term)
        .at[send_index]
        .add(returned.reshape(-1, channels).astype(jnp.float32))
    )
    conv_grad = (act_grad * slope).astype(jnp.bfloat16)
    padded = with_halo(conv_grad[None], (("seq", 1),), half)[0]
    piece = lax.all_gather(conv_weight, "dp", axis=1, tiled=True)
    total = jnp.zeros((slab_len, piece.shape[1]), jnp.float32)
    for tap in range(kernel):
        window = padded[2 * half - tap : 2 * half - tap + slab_len]
        total = total + lax.dot_general(
            window, piece[tap], (((1,), (1,)), ((), ())), preferred_element_type=jnp.float32
        )
    input_grad = total.astype(jnp.bfloat16)
    pair_sum = lax.psum(pair_part, ("dp", "seq"))
    scale = 1.0 / math.sqrt(lax.axis_size("dp") * seq_count * seq_count * slot_count)
    return (input_grad[None], pair_sum * scale)


MESH = pl.DeviceIdType.MESH
NZ, NY, NC = 4, 2, 2
PEERS = NZ * NY
CHUNKS = 4
FINISH_PARTS = 4
AG_ORDER = (2, 4, 6)
SEND_ORDER = (2, 3, 1, 4, 5, 6, 7)
TAP_PARTS = ((0, 3), (3, 2))
ROWS_T = (((0,), (0,)), ((), ()))
COLS_T = (((1,), (1,)), ((), ()))


def dot(a, b):
    return jnp.dot(a, b, preferred_element_type=jnp.float32)


def dot_t(a, b, dims):
    return lax.dot_general(a, b, dims, preferred_element_type=jnp.float32)


def kernel(
    pre_hbm, trunk_hbm, w_ref, p_hbm, ds_hbm, as_hbm, jg_hbm, pc_hbm,
    out_ref, final,
    pre_s, p_s, ds_s, as_s, jg_s, pc_s, in_sem,
    act_s, slope_s, idx_send, idx_recv, drows, weighted, zbuf, pad_s, wbuf,
    c_send, c_recv, own_s, r_send, r_recv, r_done, o_send, o_all, perm_s,
    wz_s, wz_r, wy_s, wy_r, wc_s, wc_r, xs_s, xs_r, cc_s, cc_r,
    rs_s, rs_r, ag_s, ag_r, xf_s, xf_r, ready,
):
    dp = lax.axis_index("dp")
    x = lax.axis_index("seq")
    c = dp % 2
    y = (dp // 2) % 2
    z = dp // 4
    me8 = dp // 2
    ox = 1 - x
    oc = 1 - c
    slab, chan = pre_s.shape[1:]
    slots = ds_s.shape[-1]
    taps, shard = w_ref.shape[:2]
    hc = chan // 2
    tok = slab // 2
    piece = hc // PEERS
    line = NZ * shard
    first = x == 0

    def half(index):
        return pl.ds(pl.multiple_of(index * hc, 128), hc)

    mine, theirs = half(x), half(ox)

    def dev(zz, yy, cc):
        return (zz * NY + yy) * NC + cc

    xdev = (dp, ox)
    cdev = (me8 * 2 + oc, x)
    ydev = (dev(z, 1 - y, c), x)

    def zdev(d):
        return (dev(z + 1 if d == 0 else z - 1, y, c), x)

    def has_next(d):
        return z < NZ - 1 if d == 0 else z > 0

    relays = c == x

    def wpart(zz, yy, part):
        start, count = TAP_PARTS[part]
        return wbuf.at[pl.ds(start, count), pl.ds(pl.multiple_of((yy * NZ + zz) * shard, 16), shard), :]

    def w_own(part):
        start, count = TAP_PARTS[part]
        return w_ref.at[pl.ds(start, count)]

    own_w = pltpu.make_async_copy(
        w_ref, wbuf.at[:, pl.ds(pl.multiple_of((y * NZ + z) * shard, 16), shard), :], in_sem.at[8])

    def tokens(s):
        return trunk_hbm.at[0, pl.ds(pl.multiple_of((ox if s else x) * tok, 16), tok), :]

    loads = [
        pltpu.make_async_copy(src, dst, in_sem.at[i])
        for i, (src, dst) in enumerate([
            (ds_hbm, ds_s), (as_hbm, as_s), (jg_hbm, jg_s), (pc_hbm, pc_s),
            (pre_hbm.at[0], pre_s.at[0]),
            (p_hbm, p_s),
            (tokens(0), zbuf.at[0, 4 * slots :, mine]), (tokens(1), zbuf.at[1, 4 * slots :, mine])])
    ]
    for cp in loads:
        cp.start()

    @pl.when(relays)
    def _():
        own_w.start()

    barrier = pltpu.get_barrier_semaphore()
    for target in (xdev, cdev, ydev):
        pl.semaphore_signal(barrier, inc=1, device_id=target, device_id_type=MESH)
    for d in range(2):
        @pl.when(has_next(d))
        def _(d=d):
            pl.semaphore_signal(barrier, inc=1, device_id=zdev(d), device_id_type=MESH)

    def remote(src, dst, ss, rs, target):
        return pltpu.make_async_remote_copy(
            src_ref=src, dst_ref=dst, send_sem=ss, recv_sem=rs,
            device_id=target, device_id_type=MESH,
        )

    edge = jnp.where((z == 0) | (z == NZ - 1), 4, 5)
    pl.semaphore_wait(barrier, edge)

    rows_c = slab // CHUNKS
    pre_copies = [
        remote(pre_hbm.at[0, k * rows_c : (k + 1) * rows_c, :],
               pre_s.at[1, k * rows_c : (k + 1) * rows_c, :], xs_s.at[1 + k], xs_r.at[1 + k], xdev)
        for k in range(CHUNKS)]
    trunk_copies = [
        remote(tokens(1 - s), zbuf.at[s, 4 * slots :, mine],
               xs_s.at[2 + CHUNKS + s], xs_r.at[2 + CHUNKS + s], xdev)
        for s in range(2)]
    for cp in pre_copies[:1]:
        cp.start()

    hops = [(d, s) for s in range(NZ - 1) for d in range(2)]

    def entry(hop):
        return 0 if hop is None else 1 + hop[0] * 3 + hop[1]

    def source_z(hop):
        if hop is None:
            return z
        return z - 1 - hop[1] if hop[0] == 0 else z + 1 + hop[1]

    def when(hop, body):
        if hop is None:
            pl.when(relays)(body)
        else:
            pl.when(relays & (source_z(hop) >= 0 if hop[0] == 0 else source_z(hop) < NZ))(body)

    def z_copy(d, s, part):
        block = wpart(z - s if d == 0 else z + s, y, part)
        sem = 2 * (d * 3 + s) + part
        return remote(block if s else w_own(part), block, wz_s.at[sem], wz_r.at[sem], zdev(d))

    def z_arrival(d, s, part):
        block = wpart(source_z((d, s)), y, part)
        sem = 2 * (d * 3 + s) + part
        return remote(block, block, wz_s.at[sem], wz_r.at[sem], ydev)

    def y_copy(hop, part, arriving=False):
        block = wpart(source_z(hop), 1 - y if arriving else y, part)
        src = w_own(part) if hop is None and not arriving else block
        sem = 2 * entry(hop) + part
        return remote(src, block, wy_s.at[sem], wy_r.at[sem], ydev)

    def core_copy(kind, hop, part):
        block = wpart(source_z(hop), 1 - y if kind else y, part)
        src = w_own(part) if kind == 0 and hop is None else block
        sem = 2 * (kind * 7 + entry(hop)) + part
        return remote(src, block, wc_s.at[sem], wc_r.at[sem], cdev)

    for part in range(2):
        for d in range(2):
            @pl.when(relays & has_next(d))
            def _(d=d, part=part):
                z_copy(d, 0, part).start()

        @pl.when(relays)
        def _(part=part):
            y_copy(None, part).start()
            core_copy(0, None, part).start()

    def say(stage):
        for d in range(2):
            @pl.when(has_next(d))
            def _(d=d):
                pl.semaphore_signal(
                    ready.at[stage * 2 + d], inc=1, device_id=zdev(d), device_id_type=MESH)

    def hear(stage):
        for d in range(2):
            @pl.when(has_next(1 - d))
            def _(d=d):
                pl.semaphore_wait(ready.at[stage * 2 + d], 1)

    for cp in loads[:4]:
        cp.wait()

    def ordered(rows):
        a, b = rows[0:1], rows[1:2]
        return [jnp.where(first, a, b), jnp.where(first, b, a)]

    d_own = ordered(ds_s[0, 0].astype(jnp.float32))
    a_own = ordered(as_s[0, 0].astype(jnp.float32))
    counts = pc_s[0]
    cnt = jnp.where(first, counts[:, 0:1], counts[:, 1:2])
    live = lax.broadcasted_iota(jnp.int32, (2, slots), 1) < cnt
    jw_own = ordered(jnp.where(live, jg_s[0, 0], 0.0))
    nothing = jnp.zeros((2, slots), jnp.float32)
    idx_send[...] = jnp.concatenate(d_own + a_own + jw_own + [nothing], axis=0)

    idx_copy = remote(idx_send, idx_recv, xs_s.at[0], xs_r.at[0], xdev)
    idx_copy.start()
    for cp in pre_copies[1:]:
        cp.start()
    say(0)

    def pass_z(s, part):
        for d in range(2):
            def body(d=d):
                z_arrival(d, s, part).wait_recv()
                if s < NZ - 2:
                    @pl.when(has_next(d))
                    def _():
                        z_copy(d, s + 1, part).start()
                y_copy((d, s), part).start()
                core_copy(0, (d, s), part).start()
            when((d, s), body)

    def pass_y(step, part):
        for hop in [None] if step == 0 else [(0, step - 1), (1, step - 1)]:
            def body(hop=hop):
                y_copy(hop, part, True).wait_recv()
                core_copy(1, hop, part).start()
            when(hop, body)

    def gelu(s, start, count):
        rows = slice(start, start + count)
        values = pre_s[s, rows, :].astype(jnp.float32)
        normal_cdf = 0.5 * (1.0 + lax.erf(values / math.sqrt(2.0)))
        act_s[s, rows, :] = (values * normal_cdf).astype(jnp.bfloat16)
        slope_s[s, rows, :] = normal_cdf

    def finish_slope(s):
        values = pre_s[s].astype(jnp.float32)
        density = jnp.exp(-0.5 * values * values) / math.sqrt(2.0 * math.pi)
        slope_s[s] += values * density

    position = lax.broadcasted_iota(jnp.int32, (slab, 2 * slots), 0).astype(jnp.float32)

    def onehot(pair):
        return jnp.where(position == jnp.concatenate(pair, axis=1), 1.0, 0.0)

    def flip(m):
        return jnp.transpose(m).astype(jnp.bfloat16)

    def column(row):
        return jnp.transpose(jnp.broadcast_to(row, (slots, slots)))[:, 0:1]

    def block(q, r):
        return slice((2 * q + r) * slots, (2 * q + r + 1) * slots)

    def gather_donors(s, hot):
        rows = dot(flip(hot), act_s[s]).astype(jnp.bfloat16)
        for q in range(2):
            drows[block(q, s), :] = rows[q * slots : (q + 1) * slots]

    def gather_acceptors(s, hot, cols):
        rows = dot(flip(hot), act_s[s])
        for r in range(2):
            weighted[block(s, r), :] = (
                cols[r] * rows[r * slots : (r + 1) * slots]).astype(jnp.bfloat16)

    def donor_terms(q):
        term = dot_t(weighted[2 * q * slots : 2 * (q + 1) * slots, :], p_s[...], COLS_T)
        for r in range(2):
            zbuf[r, (2 + q) * slots : (3 + q) * slots, :] = (
                term[r * slots : (r + 1) * slots].astype(jnp.bfloat16))

    def accept_terms(r, cols):
        for q in range(2):
            term = dot(drows[block(q, r), :], p_s[...]) * cols[q][r]
            zbuf[q, r * slots : (r + 1) * slots, :] = term.astype(jnp.bfloat16)

    loads[4].wait()
    gelu(0, 0, slab)
    hot_d = [onehot(d_own)]
    hot_a = [onehot(a_own)]
    w_cols = [[column(w) for w in jw_own]]
    gather_donors(0, hot_d[0])
    gather_acceptors(0, hot_a[0], w_cols[0])
    hear(0)
    say(1)
    loads[5].wait()
    donor_terms(0)

    finish_slope(0)
    hear(1)
    say(2)
    def take(k):
        pre_copies[k].wait_recv()
        gelu(1, k * rows_c, rows_c)

    take(0)
    pass_z(0, 0)
    pass_z(0, 1)
    take(1)
    for cp in trunk_copies:
        cp.start()
    pass_z(1, 0)
    hear(2)
    take(2)
    idx_copy.wait_recv()
    got = idx_recv[...]
    hot_d.append(onehot([got[1:2], got[0:1]]))
    hot_a.append(onehot([got[3:4], got[2:3]]))
    w_cols.append([column(got[5:6]), column(got[4:5])])
    accept_terms(0, w_cols)
    pass_z(1, 1)
    take(3)
    gather_acceptors(1, hot_a[1], w_cols[1])
    gather_donors(1, hot_d[1])
    c_send[...] = dot_t(drows[:, mine], weighted[:, half(oc)], ROWS_T).astype(jnp.bfloat16)
    c_copy = remote(c_send, c_recv, cc_s.at[0], cc_r.at[0], cdev)
    c_copy.start()
    own_s[...] = dot_t(drows[:, mine], weighted[:, half(c)], ROWS_T)
    c_copy.wait_recv()
    own_s[...] += c_recv[...].astype(jnp.float32)
    r_send[...] = own_s[...].astype(jnp.bfloat16)

    def peer8(k):
        zz = [z, z + 1 - 2 * (z % 2), lax.rem(z + 2, NZ), NZ - 1 - z][k // 2]
        return zz * NY + (1 - y if k % 2 else y)

    rs = {}
    for k in SEND_ORDER:
        to = peer8(k)
        rs[k] = remote(r_send.at[pl.ds(pl.multiple_of(to * piece, 16), piece), :], r_recv.at[k - 1],
                       rs_s.at[k - 1], rs_r.at[k - 1], (to * 2 + c, x))
        rs[k].start()

    pass_z(2, 0)
    pass_y(0, 0)
    pass_y(0, 1)
    donor_terms(1)
    accept_terms(1, w_cols)
    finish_slope(1)
    pass_z(2, 1)
    pass_y(1, 0)
    pass_y(1, 1)
    for cp in loads[6:8]:
        cp.wait()
    for cp in trunk_copies:
        cp.wait_recv()
    spread = jnp.where(
        lax.broadcasted_iota(jnp.int32, (slab, tok), 0) // 2
        == lax.broadcasted_iota(jnp.int32, (slab, tok), 1), 0.5, 0.0)
    zeros = jnp.zeros((8, chan), jnp.float32)
    for s in range(2):
        scatter = jnp.concatenate([hot_a[s], hot_d[s], spread], axis=1).astype(jnp.bfloat16)
        grad = dot(scatter, zbuf[s]) * slope_s[s]
        grad = grad.astype(jnp.bfloat16).astype(jnp.float32)
        pad_s[s, 8 : 8 + slab, :] = grad
        head, tail = grad[0:8], grad[slab - 8 : slab]
        own_first = first if s == 0 else jnp.logical_not(first)
        pad_s[1 - s, 0:8, :] = jnp.where(own_first, tail, zeros)
        pad_s[1 - s, 8 + slab :, :] = jnp.where(own_first, zeros, head)

    @pl.when(relays)
    def _():
        own_w.wait()

    def lines_in(kind):
        for hop in [None] + hops:
            ok = (z >= 0) if hop is None else source_z(hop) >= 0 if hop[0] == 0 else source_z(hop) < NZ

            def run(hop=hop):
                for part in range(2):
                    core_copy(kind, hop, part).wait_recv()
            pl.when(jnp.logical_not(relays) & ok)(run)

    shift = taps // 2

    def conv(s, yy):
        acc = None
        for tap in range(taps):
            window = pad_s[s, 8 + shift - tap : 8 + shift - tap + slab, :].astype(jnp.bfloat16)
            term = dot_t(window, wbuf[tap, pl.ds(pl.multiple_of(yy * line, 16), line), :], COLS_T)
            acc = term if acc is None else acc + term
        return acc.astype(jnp.bfloat16)

    def give(kind):
        yy = 1 - y if kind else y
        o_send[kind] = conv(1, yy)
        cp = remote(o_send.at[kind], o_all.at[2 * x + yy],
                    xs_s.at[4 + CHUNKS + kind], xs_r.at[4 + CHUNKS + kind], xdev)
        cp.start()
        return cp

    lines_in(0)
    o_copies = [give(0)]
    target = lax.broadcasted_iota(jnp.int32, (chan, 1), 0)
    part_of, target = target // hc, target % hc
    line_of, target = target // line, target % line
    target = (target // shard * NY + line_of) * (NC * shard) + part_of * shard + target % shard
    perm_s[...] = jnp.where(
        lax.broadcasted_iota(jnp.int32, (chan, chan), 1) == target, 1.0, 0.0).astype(jnp.bfloat16)
    pass_y(2, 0)
    pass_y(2, 1)
    for k in range(1, PEERS):
        rs[k].wait_recv()
    total = own_s[pl.ds(pl.multiple_of(me8 * piece, 8), piece), :]
    for k in range(PEERS - 1):
        total = total + r_recv[k].astype(jnp.float32)
    r_done[...] = total.astype(jnp.bfloat16)

    def fblock(xx, index, count=1):
        return final.at[pl.ds(pl.multiple_of(xx * hc + index * piece, 16), count * piece), half(c)]

    place = pltpu.make_async_copy(r_done, fblock(x, me8), in_sem.at[9])
    place.start()
    ag = {}
    for k in AG_ORDER:
        ag[k] = remote(r_done, fblock(x, me8), ag_s.at[k // 2 - 1], ag_r.at[k // 2 - 1], (peer8(k) * 2 + c, x))
        ag[k].start()
    xf = []

    def forward(k, src):
        for n, to in enumerate([(dev(z, 1 - y, c), ox), xdev, ydev]):
            cp = remote(src, fblock(x, peer8(k)), xf_s.at[2 * k + n], xf_r.at[2 * k + n], to)
            cp.start()
            xf.append(cp)

    forward(0, r_done)

    pass_y(3, 0)
    pass_y(3, 1)
    lines_in(1)
    o_copies.append(give(1))
    for k in (2, 4, 6):
        ag[k].wait_recv()
        forward(k, fblock(x, peer8(k)))
    place.wait()
    for cp in xf[2::3]:
        cp.wait_recv()
    quarter = fblock(x, 0, PEERS)
    cq = remote(quarter, quarter, cc_s.at[1], cc_r.at[1], cdev)
    cq.start()
    for yy in range(NY):
        o_all[2 * x + yy] = conv(0, yy)
    for cp in o_copies:
        cp.wait_recv()
    out_ref[0] = sum(
        dot(o_all[k], perm_s[k * line : (k + 1) * line, :]) for k in range(2 * NY)
    ).astype(jnp.bfloat16)
    late = []
    for k in (0, 2, 4, 6):
        for n in (1, 0):
            xf[3 * (k // 2) + n].wait_recv()
            part = fblock(ox, peer8(k if n else k + 1))
            cp = remote(part, part, cc_s.at[2 + len(late)], cc_r.at[2 + len(late)], cdev)
            cp.start()
            late.append(cp)
    cq.wait_recv()
    for cp in late:
        cp.wait_recv()
    for hop in [None] + hops:
        def sent(hop=hop):
            for part in range(2):
                y_copy(hop, part).wait_send()
                for kind in range(2):
                    core_copy(kind, hop, part).wait_send()
        when(hop, sent)
    for d in range(2):
        for s in range(NZ - 1):
            leaves = (z < NZ - 1) & (z >= s) if d == 0 else (z > 0) & (z + s < NZ)
            @pl.when(relays & leaves)
            def _(d=d, s=s):
                for part in range(2):
                    z_copy(d, s, part).wait_send()
    for cp in [idx_copy, c_copy, cq] + late + o_copies + pre_copies + trunk_copies + list(rs.values()) + list(ag.values()) + xf:
        cp.wait_send()


def finish(scale, grad_ref, final, out_hbm, pair_hbm, scaled, sem):
    copies = [pltpu.make_async_copy(grad_ref, out_hbm, sem.at[0])]
    copies[0].start()
    rows = final.shape[0] // FINISH_PARTS
    for k in range(FINISH_PARTS):
        part = slice(k * rows, (k + 1) * rows)
        scaled[part, :] = final[part, :].astype(jnp.float32) * scale
        copies.append(pltpu.make_async_copy(scaled.at[part, :], pair_hbm.at[part, :], sem.at[k + 1]))
        copies[-1].start()
    for cp in copies:
        cp.wait()


def per_device_kernel(pre_act, trunk_grad, conv_weight, pair_weight, donor_slots, accept_slots, junction_grad, pair_counts):
    slab, chan = pre_act.shape[1:]
    slots = donor_slots.shape[3]
    taps = conv_weight.shape[0]
    hc = chan // 2
    piece = hc // PEERS
    bf, f32 = jnp.bfloat16, jnp.float32
    V = pltpu.VMEM
    D = pltpu.SemaphoreType.DMA
    scratch = [
        V((2, slab, chan), bf), V((chan, chan), bf), V(donor_slots.shape, jnp.int32),
        V(accept_slots.shape, jnp.int32), V(junction_grad.shape, f32), V(pair_counts.shape, jnp.int32),
        D((10,)),
        V((2, slab, chan), bf), V((2, slab, chan), f32), V((8, slots), f32), V((8, slots), f32),
        V((4 * slots, chan), bf), V((4 * slots, chan), bf), V((2, 4 * slots + slab // 2, chan), bf),
        V((2, slab + 16, chan), f32), V((taps, hc, chan), bf),
        V((hc, hc), bf), V((hc, hc), bf), V((hc, hc), f32), V((hc, hc), bf),
        V((PEERS - 1, piece, hc), bf), V((piece, hc), bf),
        V((NY, slab, hc // NY), bf), V((2 * NY, slab, hc // NY), bf), V((chan, chan), bf),
        D((12,)), D((12,)), D((14,)), D((14,)), D((28,)), D((28,)),
        D((6 + CHUNKS,)), D((6 + CHUNKS,)), D((2 + PEERS,)), D((2 + PEERS,)),
        D((PEERS - 1,)), D((PEERS - 1,)), D((NZ - 1,)), D((NZ - 1,)), D((2 * PEERS,)), D((2 * PEERS,)),
        pltpu.SemaphoreType.REGULAR((6,)),
    ]
    done = pl.pallas_call(
        kernel,
        out_shape=(jax.ShapeDtypeStruct(pre_act.shape, bf), jax.ShapeDtypeStruct((chan, chan), bf)),
        in_specs=[pl.BlockSpec(memory_space=pltpu.HBM)] * 8,
        out_specs=[pl.BlockSpec(memory_space=pltpu.VMEM)] * 2,
        scratch_shapes=scratch,
        compiler_params=pltpu.CompilerParams(
            collective_id=0, has_side_effects=True, vmem_limit_bytes=40 << 20),
    )(*[
        pltpu.with_memory_space_constraint(a, pltpu.HBM)
        for a in (pre_act, trunk_grad, conv_weight, pair_weight, donor_slots, accept_slots,
                  junction_grad, pair_counts)
    ])
    scale = 1.0 / math.sqrt(NZ * NY * NC * 2 * 2 * slots)
    return pl.pallas_call(
        functools.partial(finish, scale),
        out_shape=(jax.ShapeDtypeStruct(pre_act.shape, bf), jax.ShapeDtypeStruct((chan, chan), f32)),
        in_specs=[pl.BlockSpec(memory_space=pltpu.VMEM)] * 2,
        out_specs=[pl.BlockSpec(memory_space=pltpu.HBM)] * 2,
        scratch_shapes=[V((chan, chan), f32), D((FINISH_PARTS + 1,))],
    )(*[pltpu.with_memory_space_constraint(a, pltpu.VMEM) for a in done])


def solution(mesh):
    in_specs = (
        P("dp", "seq", None),
        P("dp", None, "seq"),
        P(None, "dp", None),
        P(),
        P("dp", "seq", None, None),
        P("dp", "seq", None, None),
        P("dp", "seq", None, None),
        P("dp", None, None),
    )
    out_specs = (P("dp", "seq", None), P())
    fits = mesh.shape["dp"] == NZ * NY * NC and mesh.shape["seq"] == 2
    return jax.shard_map(
        per_device_kernel if fits else per_device_general, mesh=mesh, in_specs=in_specs, out_specs=out_specs, check_vma=False
    )
```
